32 devices in a mesh: dp: 4 (over y, x), expert: 4 (over z), tensor: 2 (over core).
Axes of the slice: x: 2, y: 2, z: 4, core: 2. Of those that a mesh axis runs over, the one named last changes fastest.
Arguments:
- tokens: bfloat16 [2048, 7168], P(('dp', 'expert'), 'tensor'), may hold values from -6 to 6
- routing: int32 [2048, 2], P(('dp', 'expert')), may hold values from 0 to 3, all different within a row; in each aligned block of 128 rows (0 to 127, 128 to 255, ...) at most 72 rows name the same one
- gate_values: float32 [2048, 2], P(('dp', 'expert')), may hold values from 0.1 to 1
- expert_weight: bfloat16 [4, 7168, 1024], P('expert', 'tensor'), may hold values from -0.0625 to 0.0625
- subspace: bfloat16 [4, 64, 7168], P('expert', None, 'tensor'), may hold values from -0.0625 to 0.0625
- gradient: float32 [4, 2, 3584, 1024], P('expert', 'tensor', 'dp'), may hold values from -6 to 6
Outputs:
- combined: bfloat16 [2048, 1024], P(('dp', 'expert'), 'tensor')
- new_basis: float32 [4, 2, 64, 3584], P('expert', 'tensor', None, 'dp')
- preconditioned: float32 [4, 2, 3584, 1024], P('expert', 'tensor', 'dp')
The draws below stay inside these ranges and needn't reach their ends.
Inputs may be any that keep to these rules, and one draw needn't show every extreme that they name: `routing`: each row names 2 different experts; in each device's aligned block of 128 rows no expert is named more than 72 times, a bound that some block reaches.
All inputs are finite; a program needn't handle non-finite values.
Results may differ from the reference program's by a relative error of at most 0.0049.
Values may be sent and summed in bfloat16 or wider, within the bound.
A program may use at most 64 MiB of HBM per device.

```python
import math
import jax
import jax.numpy as jnp
import numpy as np
from jax import lax

D = 7168
FF = 1024
RANK = 64
BLOCKS = 2
TOPK = 2
TOK_DEV = 128
EXPERTS = 4
CAP = 72
TOKENS = 2048
N_DP = 4
N_EXPERT = 4


def shard_levels(key, shape, pieces, least, top_value):
    def one(axis_at, shards_of):
        steps = jax.random.uniform(jax.random.fold_in(jax.random.fold_in(key, 6), axis_at), (shards_of,), jnp.float32, least / len(pieces), top_value / len(pieces))
        return jnp.repeat(jnp.exp(steps), shape[axis_at] // shards_of).reshape((-1,) + (1,) * (len(shape) - axis_at - 1))

    level = one(*pieces[0])
    for cut in pieces[1:]:
        level = level * one(*cut)
    return level


def shared_out(stream_key, own, number, rows, count, top, limit, skew):
    ranking = jax.random.permutation(stream_key, count)
    heavy_load, common = shares(count, rows * top, limit, skew, True), shares(count, rows * top, limit, skew, False)
    places = jnp.arange(count)

    def named(tallies, rotation):
        used = int((tallies > 0).sum())
        fixed = max(1, used // 4)
        shifted = fixed + (places - fixed + rotation * (used - fixed)) % max(1, count - fixed)
        return jnp.zeros((count,), jnp.int32).at[ranking[jnp.where(places < fixed, places, shifted)]].set(jnp.asarray(tallies, jnp.int32))

    tallies = jnp.where(number % 4 == 0, named(heavy_load, number // 4), named(common, number - number // 4 - 1))
    mixed = jax.random.permutation(jax.random.fold_in(own, 3), count)
    giver, receiver = mixed[0:count // 2 * 2:2], mixed[1:count // 2 * 2:2]
    margin = jnp.minimum(tallies[giver] - 1, limit - tallies[receiver]) // 2
    margin = jnp.where((giver == ranking[0]) | (receiver == ranking[0]) | (tallies[receiver] == 0), 0, jnp.maximum(margin, 0))
    shifted = jax.random.randint(jax.random.fold_in(own, 4), (count // 2,), 0, 1 << 20) % (margin + 1)
    tallies = tallies.at[giver].add(-shifted).at[receiver].add(shifted)
    labels = jnp.searchsorted(jnp.cumsum(tallies), jnp.arange(rows * top), side="right").astype(jnp.int32)
    listing = labels.reshape(top, rows).T
    listing = listing[jax.random.permutation(jax.random.fold_in(own, 1), rows)]
    rotation = jax.random.randint(jax.random.fold_in(own, 2), (rows, 1), 0, top)
    return jnp.take_along_axis(listing, (jnp.arange(top)[None, :] + rotation) % top, axis=1)


def shares(count, total, limit, lean, full):
    weights = [(1 << 20) // math.isqrt(rank ** lean) + 1 for rank in range(1, count + 1)]
    largest = limit if full else min(limit, max(-(-total // count), total * weights[0] // sum(weights)))
    least = 1 if total - largest >= count - 1 else 0
    holding, surplus = [largest] + [least] * (count - 1), total - largest - least * (count - 1)
    while surplus > 0:
        free = [i for i in range(1, count) if holding[i] < largest] or [i for i in range(1, count) if holding[i] < limit]
        whole, budget = sum([weights[i] for i in free]), surplus
        for i in free:
            addition = min(limit - holding[i], max(1, budget * weights[i] // whole), surplus)
            holding[i] = holding[i] + addition
            surplus = surplus - addition
    return np.array(holding)


def gaussian(stream_key, dims, width, bound, shards=(), kind=jnp.bfloat16):
    array = jax.random.normal(stream_key, dims, jnp.float32) * width
    if len(shards) > 0:
        array = shard_levels(stream_key, dims, shards, -0.22, 0.18) * array
    return jnp.clip(array, min=-bound, max=bound).astype(kind)


def setup_inputs(seed: int = 0) -> dict:
    key_of = jax.random.split(jax.random.key(seed), 7)
    tokens = gaussian(key_of[0], (TOKENS, D), 1.0, 6.0, ((0, 16), (1, 2)))
    routing_keys = jax.random.split(jax.random.fold_in(key_of[1], 1), TOKENS // TOK_DEV)
    routing_turns = jax.random.permutation(jax.random.fold_in(key_of[1], 3), TOKENS // TOK_DEV)
    routing = jax.vmap(lambda own, number: shared_out(jax.random.fold_in(key_of[1], 2), own, number, TOK_DEV, EXPERTS, TOPK, CAP, 2))(routing_keys, routing_turns).reshape((TOKENS, TOPK))
    gate_values = jnp.clip(0.1 + 0.9 * jax.random.uniform(key_of[2], (TOKENS, TOPK), jnp.float32) ** shard_levels(key_of[2], (TOKENS, TOPK), ((0, 16),), -0.2, 0.2), 0.1, 1.0)
    expert_weight = gaussian(key_of[3], (EXPERTS, D, FF), D ** -0.5, 0.0625, ((0, 4), (1, 2)))
    subspace = gaussian(key_of[4], (EXPERTS, RANK, D), D ** -0.5, 0.0625, ((0, 4), (2, 2)))
    gradient = gaussian(key_of[5], (EXPERTS, BLOCKS, D // BLOCKS, FF), 1.0, 6.0, ((0, 4), (1, 2), (2, 4)), jnp.float32)
    return dict(tokens=tokens, routing=routing, gate_values=gate_values, expert_weight=expert_weight, subspace=subspace, gradient=gradient)


EPSILON = 1e-05

def tri_solve(factor, rhs, flip):
    return lax.linalg.triangular_solve(factor, rhs, left_side=True, lower=True, transpose_a=flip)

def precondition(image_rows, square_sums, grad_rows, token_mean):
    highest = lax.Precision.HIGHEST
    diagonal = square_sums / token_mean + EPSILON
    gram_matrix = jnp.dot(image_rows, image_rows.T, precision=highest)
    factor_low = jnp.linalg.cholesky(gram_matrix)
    eigen_scale = jnp.diagonal(factor_low) / token_mean
    scaled = image_rows / diagonal[None, :]
    middle = jnp.dot(factor_low / eigen_scale[None, :], factor_low.T, precision=highest)
    middle = middle + jnp.dot(scaled, image_rows.T, precision=highest)
    inner_term = jnp.dot(scaled, grad_rows, precision=highest)
    factor_mid = jnp.linalg.cholesky(middle)
    solved = tri_solve(factor_mid, tri_solve(factor_mid, inner_term, False), True)
    result = grad_rows / diagonal[:, None] - jnp.dot(scaled.T, solved, precision=highest)
    basis_out = tri_solve(factor_low, image_rows, False)
    return (basis_out, result)

def reference(tokens, routing, gate_values, expert_weight, subspace, gradient):
    half_width = D // BLOCKS
    pair_count = TOKENS * TOPK
    most_rows = N_DP * N_EXPERT * CAP
    token_mean = float(TOKENS * TOPK) / float(EXPERTS)
    flat_ids = routing.reshape(-1)
    flat_gates = gate_values.reshape(-1)

    def per_expert(totals, expert_id):
        selected = jnp.nonzero(flat_ids == expert_id, size=most_rows, fill_value=pair_count)[0].astype(jnp.int32)
        token_ids = jnp.where(selected < pair_count, selected // TOPK, TOKENS).astype(jnp.int32)
        gate_slot = flat_gates.at[selected].get(mode='fill', fill_value=0.0)
        expert_rows = tokens.at[token_ids].get(mode='fill', fill_value=0)
        hidden = jnp.zeros((most_rows, FF), jnp.float32)
        images = []
        squares = []
        for block_id in range(BLOCKS):
            lo_col = block_id * half_width
            block_rows = expert_rows[:, lo_col:lo_col + half_width]
            partial_value = jnp.dot(block_rows.astype(jnp.float32), expert_weight[expert_id, lo_col:lo_col + half_width].astype(jnp.float32), preferred_element_type=jnp.float32)
            hidden = hidden + partial_value.astype(jnp.bfloat16).astype(jnp.float32)
            basis_block = subspace[expert_id][:, lo_col:lo_col + half_width]
            projected = lax.dot_general(block_rows.astype(jnp.float32), basis_block.astype(jnp.float32), (((1,), (1,)), ((), ())), preferred_element_type=jnp.float32).astype(jnp.bfloat16)
            images.append(lax.dot_general(projected.astype(jnp.float32), block_rows.astype(jnp.float32), (((0,), (0,)), ((), ())), preferred_element_type=jnp.float32))
            squares.append(jnp.sum(jnp.square(block_rows.astype(jnp.float32)), axis=0))
        totals = totals.at[token_ids].add(gate_slot[:, None] * hidden, mode='drop')
        return (totals, (jnp.stack(images), jnp.stack(squares)))
    totals, (image_all, square_all) = lax.scan(per_expert, jnp.zeros((TOKENS, FF), jnp.float32), jnp.arange(EXPERTS, dtype=jnp.int32))
    combined = totals.astype(jnp.bfloat16)
    inner_map = jax.vmap(lambda image_rows, square_sums, grad_rows: precondition(image_rows, square_sums, grad_rows, token_mean))
    new_basis, preconditioned = jax.vmap(inner_map)(image_all, square_all, gradient)
    return (combined, new_basis, preconditioned)
```

```python
import functools

import jax
import jax.numpy as jnp
from jax import lax
from jax.experimental import pallas as pl
from jax.experimental.pallas import tpu as pltpu
from jax.sharding import PartitionSpec as P

EPSILON = 1e-05


def tri_solve(factor, rhs, flip):
    return lax.linalg.triangular_solve(factor, rhs, left_side=True, lower=True, transpose_a=flip)


def finish(image_mine, diagonal, grad_rows, gram_matrix, curvature, inner_term, token_mean):
    highest = lax.Precision.HIGHEST
    factor_low = jnp.linalg.cholesky(gram_matrix)
    eigen_scale = jnp.diagonal(factor_low) / token_mean
    middle = jnp.dot(factor_low / eigen_scale[None, :], factor_low.T, precision=highest) + curvature
    factor_mid = jnp.linalg.cholesky(middle)
    solved = tri_solve(factor_mid, tri_solve(factor_mid, inner_term, False), True)
    scaled = image_mine / diagonal[None, :]
    result = grad_rows / diagonal[:, None] - jnp.dot(scaled.T, solved, precision=highest)
    basis_out = tri_solve(factor_low, image_mine, False)
    return (basis_out, result)


def body(tokens, routing, gate_values, expert_weight, subspace, gradient):
    highest = lax.Precision.HIGHEST
    tok_rows, half_width = tokens.shape
    choose_count = routing.shape[1]
    owners = lax.axis_size("expert")
    tensor_count = lax.axis_size("tensor")
    capacity = tok_rows * choose_count // owners * 9 // 8
    pair_count = tok_rows * choose_count
    slot_count = owners * capacity
    hidden_units = expert_weight.shape[2]
    flat_ids = routing.reshape(pair_count)
    one_hot = (flat_ids[:, None] == jnp.arange(owners, dtype=jnp.int32)[None, :]).astype(
        jnp.float32
    )
    pair_index = jnp.arange(pair_count, dtype=jnp.int32)
    strict_lower = (pair_index[:, None] > pair_index[None, :]).astype(jnp.float32)
    before = jnp.dot(strict_lower, one_hot, preferred_element_type=jnp.float32)
    position = jnp.sum(before * one_hot, axis=1).astype(jnp.int32)
    slot_ids = flat_ids * capacity + position
    matches = (jnp.arange(slot_count, dtype=jnp.int32)[:, None] == slot_ids[None, :]).reshape(
        slot_count, tok_rows, choose_count
    )
    picker = jnp.sum(matches.astype(jnp.float32), axis=2).astype(jnp.bfloat16)
    outgoing = jnp.dot(picker, tokens, preferred_element_type=jnp.float32).astype(jnp.bfloat16)
    outgoing = outgoing.reshape(owners, capacity, half_width)
    incoming = lax.all_to_all(outgoing, "expert", split_axis=0, concat_axis=0, tiled=True)
    slab_rows = incoming.reshape(slot_count, half_width)
    partial_value = jnp.dot(slab_rows, expert_weight[0], preferred_element_type=jnp.float32).astype(
        jnp.bfloat16
    )
    shaped = partial_value.reshape(owners, capacity, tensor_count, hidden_units // tensor_count)
    returned = lax.all_to_all(
        lax.all_to_all(shaped, "expert", split_axis=0, concat_axis=0, tiled=True),
        "tensor",
        split_axis=2,
        concat_axis=2,
        tiled=True,
    )
    hidden = jnp.sum(returned.astype(jnp.float32), axis=2).reshape(
        slot_count, hidden_units // tensor_count
    )
    weighting = jnp.sum(matches.astype(jnp.float32) * gate_values[None, :, :], axis=2).T
    combined = jnp.dot(weighting, hidden, precision=highest).astype(jnp.bfloat16)
    projected = lax.dot_general(
        slab_rows, subspace[0], (((1,), (1,)), ((), ())), preferred_element_type=jnp.float32
    ).astype(jnp.bfloat16)
    image_rows = lax.dot_general(
        projected, slab_rows, (((0,), (0,)), ((), ())), preferred_element_type=jnp.float32
    )
    square_sums = jnp.sum(jnp.square(slab_rows.astype(jnp.float32)), axis=0)
    stacked = jnp.concatenate([image_rows, square_sums[None, :]], axis=0)
    rank_rows = image_rows.shape[0]
    token_mean = float(tok_rows * choose_count * lax.axis_size("dp"))
    grad_rows = gradient[0, 0]
    summed = lax.psum_scatter(stacked, "dp", scatter_dimension=1, tiled=True)
    image_mine = summed[:rank_rows]
    diagonal = summed[rank_rows] / token_mean + EPSILON
    scaled = image_mine / diagonal[None, :]
    gram_part = jnp.dot(image_mine, image_mine.T, precision=highest)
    curve_part = jnp.dot(scaled, image_mine.T, precision=highest)
    inner_part = jnp.dot(scaled, grad_rows, precision=highest)
    gram_matrix, curvature, inner_term = lax.psum((gram_part, curve_part, inner_part), "dp")
    basis_out, result = finish(
        image_mine, diagonal, grad_rows, gram_matrix, curvature, inner_term, token_mean
    )
    return (combined, basis_out[None, None], result[None, None])


HIGHEST = lax.Precision.HIGHEST
MESH = pl.DeviceIdType.MESH


def is_power(n):
    return n & (n - 1) == 0


def fits(sizes, tokens, subspace, gradient, expert_weight):
    few = sizes["dp"] <= 4 and sizes["expert"] <= 4 and sizes["tensor"] == 2
    even = is_power(sizes["dp"]) and is_power(sizes["expert"])
    lanes = gradient.shape[2] % 128 == 0 and expert_weight.shape[2] % 256 == 0
    return few and even and lanes and subspace.shape[1] == 64 and tokens.shape[0] == 128


def flip(index, k, n):
    out, bit = 0, 1
    while bit < n:
        own = lax.rem(index // bit, 2)
        out = out + bit * (1 - own if (k // bit) % 2 else own)
        bit *= 2
    return out


def split(x):
    high = x.astype(jnp.bfloat16)
    low = (x - high.astype(jnp.float32)).astype(jnp.bfloat16)
    return high, low


def f32_dot(a, b, dims):
    return lax.dot_general(a, b, (dims, ((), ())), preferred_element_type=jnp.float32)


def eliminate(matrix, work):
    rank = matrix.shape[0]
    row_id = lax.broadcasted_iota(jnp.int32, (rank, 2 * rank), 0)
    lane_id = lax.broadcasted_iota(jnp.int32, (rank, 2 * rank), 1)
    eye = (lax.broadcasted_iota(jnp.int32, (rank, rank), 0) == lax.broadcasted_iota(jnp.int32, (rank, rank), 1)).astype(jnp.float32)
    work[...] = jnp.concatenate([matrix, eye], axis=1)

    def step(j, state):
        row = work[pl.ds(j, 1), :]
        pivot = jnp.sum(jnp.where(lane_id[:1] == j, row, 0.0), axis=1, keepdims=True)
        column = jnp.sum(jnp.where(lane_id == j, state, 0.0), axis=1, keepdims=True)
        factor = jnp.where(row_id[:, :1] > j, column, 0.0) / pivot
        state = state - factor * row
        work[...] = state
        return state

    state = lax.fori_loop(0, rank, step, work[...])
    return state[:, :rank], state[:, rank:], jnp.sum(state[:, :rank] * eye, axis=1, keepdims=True)


def exchange(n_dp, n_exp, cap, token_mean, tok_hbm, route_ref, gate_ref, w_hbm, sub_hbm, grad_hbm,
             comb_ref, basis_ref, solved_ref, scaled_ref, recip_ref,
             tok, sub, wgt, grad, g_high, g_low, out_rows, in_rows, parts, ret, image, rs_in, small, small_in,
             inner, inner_in, work, loc_sem, tok_s, tok_r, ret_s, ret_r, rs_s, rs_r, sm_s, sm_r, in_s, in_r):
    dp = lax.axis_index("dp")
    ex = lax.axis_index("expert")
    core = lax.axis_index("tensor")
    half = parts.shape[3]
    width = tok.shape[1]
    chunk = width // n_dp
    rank = sub.shape[0]
    rows = tok.shape[0]

    loads = [
        pltpu.make_async_copy(tok_hbm, tok, loc_sem.at[0]),
        pltpu.make_async_copy(sub_hbm, sub, loc_sem.at[1]),
        pltpu.make_async_copy(w_hbm, wgt, loc_sem.at[2]),
        pltpu.make_async_copy(grad_hbm, grad, loc_sem.at[3]),
    ]
    for load in loads:
        load.start()

    barrier = pltpu.get_barrier_semaphore()
    peers = [(dp, flip(ex, k, n_exp), core) for k in range(1, n_exp)]
    peers += [(dp, flip(ex, k, n_exp), 1 - core) for k in range(n_exp)]
    peers += [(flip(dp, k, n_dp), ex, core) for k in range(1, n_dp)]
    for peer in peers:
        pl.semaphore_signal(barrier, inc=1, device_id=peer, device_id_type=MESH)

    row_i = lax.broadcasted_iota(jnp.int32, (rows, rows), 0)
    col_i = lax.broadcasted_iota(jnp.int32, (rows, rows), 1)
    earlier = (row_i < col_i).astype(jnp.float32)
    slot_i = lax.broadcasted_iota(jnp.int32, (cap, rows), 0)
    named = []
    for k in range(n_exp):
        hit = route_ref[...] == flip(ex, k, n_exp)
        named.append(jnp.sum(hit.astype(jnp.float32), axis=0, keepdims=True))
    named8 = jnp.concatenate(named + [jnp.zeros((8 - n_exp, rows), jnp.float32)], axis=0)
    before = f32_dot(named8.astype(jnp.bfloat16), earlier.astype(jnp.bfloat16), ((1,), (0,)))

    def picker(k):
        place = before[k:k + 1].astype(jnp.int32)
        return jnp.where((slot_i == place) & (named8[k:k + 1] > 0.5), 1.0, 0.0).astype(jnp.bfloat16)

    pickers = [picker(k) for k in range(n_exp)]
    loads[0].wait()
    pl.semaphore_wait(barrier, len(peers))

    sends = []

    def send(src, dst, s, r, peer):
        copy = pltpu.make_async_remote_copy(
            src_ref=src, dst_ref=dst, send_sem=s, recv_sem=r, device_id=peer, device_id_type=MESH
        )
        copy.start()
        return copy

    tok_copies = {}
    for k in list(range(n_exp - 1, 0, -1)):
        out_rows[k - 1] = f32_dot(pickers[k], tok[...], ((1,), (0,))).astype(jnp.bfloat16)
        tok_copies[k] = send(out_rows.at[k - 1], in_rows.at[k], tok_s.at[k], tok_r.at[k], (dp, flip(ex, k, n_exp), core))
    in_rows[0] = f32_dot(pickers[0], tok[...], ((1,), (0,))).astype(jnp.bfloat16)
    loads[1].wait()

    def add_image(k):
        got = in_rows.at[k]
        projected = f32_dot(got[...], sub[...], ((1,), (1,))).astype(jnp.bfloat16)
        for j in range(n_dp):
            part = got[:, j * chunk:(j + 1) * chunk]
            img = f32_dot(projected, part, ((0,), (0,)))
            wide = part.astype(jnp.float32)
            sq = jnp.sum(wide * wide, axis=0, keepdims=True)
            if k == 0:
                image[j, :rank] = img
                image[j, rank:rank + 8] = jnp.broadcast_to(sq, (8, chunk))
            else:
                image[j, :rank] += img
                image[j, rank:rank + 8] += jnp.broadcast_to(sq, (8, chunk))

    ret_copies = {}

    def project(k):
        for rel in range(2):
            which = core if rel == 0 else 1 - core
            cols = pl.ds(pl.multiple_of(which * half, half), half)
            value = f32_dot(in_rows[k], wgt[:, cols], ((1,), (0,))).astype(jnp.bfloat16)
            if k == 0 and rel == 0:
                ret[0, 0] = value
            else:
                parts[k, rel] = value
                peer = (dp, flip(ex, k, n_exp), which)
                ret_copies[k, rel] = send(parts.at[k, rel], ret.at[k, rel], ret_s.at[k, rel], ret_r.at[k, rel], peer)

    add_image(0)
    loads[2].wait()
    project(0)
    loads[3].wait()
    high, low = split(grad[...])
    g_high[...] = high
    g_low[...] = low
    order = list(range(1, n_exp))
    for k in order:
        tok_copies[k].wait_recv()
        add_image(k)
        if k != order[-1]:
            project(k)

    rs_copies = {}
    for k in range(n_dp - 1, 0, -1):
        to = flip(dp, k, n_dp)
        rs_copies[k] = send(image.at[to], rs_in.at[k], rs_s.at[k], rs_r.at[k], (to, ex, core))
    project(order[-1])
    total = image[dp]
    for k in range(1, n_dp):
        rs_copies[k].wait_recv()
        total = total + rs_in[k]
    mine = total[:rank]
    recip = 1.0 / (total[rank:rank + 1] / token_mean + EPSILON)
    scaled = mine * recip
    both = jnp.concatenate([mine, scaled], axis=0)
    small[...] = lax.dot_general(mine, both, (((1,), (1,)), ((), ())), precision=HIGHEST, preferred_element_type=jnp.float32)
    sm_copies = {}
    for k in range(n_dp - 1, 0, -1):
        sm_copies[k] = send(small, small_in.at[k], sm_s.at[k], sm_r.at[k], (flip(dp, k, n_dp), ex, core))
    s_high, s_low = split(scaled)
    s_both = jnp.concatenate([s_high, s_low], axis=0)
    cross = f32_dot(s_both, g_high[...], ((1,), (0,)))
    inner[...] = cross[:rank] + cross[rank:] + f32_dot(s_high, g_low[...], ((1,), (0,)))
    in_copies = {}
    for k in range(n_dp - 1, 0, -1):
        in_copies[k] = send(inner, inner_in.at[k], in_s.at[k], in_r.at[k], (flip(dp, k, n_dp), ex, core))
    scaled_ref[...] = scaled
    recip_ref[...] = jnp.broadcast_to(recip, (8, chunk))

    sums = small[...]
    for k in range(1, n_dp):
        sm_copies[k].wait_recv()
        sums = sums + small_in[k]
    upper, lower_inv, pivots = eliminate(sums[:, :rank], work)
    root = lax.rsqrt(pivots)
    transposed = upper * root
    basis_ref[...] = root * lax.dot_general(lower_inv, mine, (((1,), (0,)), ((), ())), precision=HIGHEST, preferred_element_type=jnp.float32)
    middle = lax.dot_general(transposed * (root * token_mean), transposed, (((0,), (0,)), ((), ())), precision=HIGHEST, preferred_element_type=jnp.float32)
    middle = middle + sums[:, rank:]
    _, mid_inv, mid_pivots = eliminate(middle, work)
    inverse = lax.dot_general(mid_inv / mid_pivots, mid_inv, (((0,), (0,)), ((), ())), precision=HIGHEST, preferred_element_type=jnp.float32)

    gates = []
    for k in range(n_exp):
        hit = (route_ref[...] == flip(ex, k, n_exp)).astype(jnp.float32)
        gates.append(jnp.sum(hit * gate_ref[...], axis=0, keepdims=True))
    gates8 = jnp.concatenate(gates + [jnp.zeros((8 - n_exp, rows), jnp.float32)], axis=0)
    gate_cols = gates8.T
    combined = jnp.zeros((rows, half), jnp.float32)
    for k in range(n_exp):
        hidden = jnp.zeros((rows, half), jnp.float32)
        for rel in range(2):
            if (k, rel) in ret_copies:
                ret_copies[k, rel].wait_recv()
            hidden = hidden + f32_dot(pickers[k], ret[k, rel], ((0,), (0,)))
        combined = combined + gate_cols[:, k:k + 1] * hidden
    comb_ref[...] = combined.astype(jnp.bfloat16)

    inner_sum = inner[...]
    for k in range(1, n_dp):
        in_copies[k].wait_recv()
        inner_sum = inner_sum + inner_in[k]
    solved_ref[...] = lax.dot_general(inverse, inner_sum, (((1,), (0,)), ((), ())), precision=HIGHEST, preferred_element_type=jnp.float32)

    for group in (tok_copies, ret_copies, rs_copies, sm_copies, in_copies):
        for copy in group.values():
            copy.wait_send()


def finish_block(grad_ref, scaled_ref, recip_ref, solved_ref, out_ref, right):
    @pl.when(pl.program_id(0) == 0)
    def _():
        v_high, v_low = split(solved_ref[...])
        right[...] = jnp.concatenate([v_high, v_low, v_high, v_low], axis=0)

    s_high, s_low = split(scaled_ref[...])
    left = jnp.concatenate([s_high, s_high, s_low, s_low], axis=0)
    fix = f32_dot(left, right[...], ((0,), (0,)))
    scale = recip_ref[...].T[:, :1]
    out_ref[...] = grad_ref[...] * scale - fix


def fast(sizes, tokens, routing, gate_values, expert_weight, subspace, gradient):
    n_dp, n_exp = sizes["dp"], sizes["expert"]
    rows, width = tokens.shape
    choices = routing.shape[1]
    cap = rows * choices // n_exp * 9 // 8
    cap = -(-cap // 8) * 8
    rank = subspace.shape[1]
    hidden = expert_weight.shape[2]
    half = hidden // 2
    chunk = width // n_dp
    token_mean = float(rows * choices * n_dp)
    f32, b16 = jnp.float32, jnp.bfloat16
    hbm = pl.BlockSpec(memory_space=pl.ANY)
    vmem = pl.BlockSpec(memory_space=pltpu.VMEM)
    dma = pltpu.SemaphoreType.DMA
    combined, basis, solved, scaled, recip = pl.pallas_call(
        functools.partial(exchange, n_dp, n_exp, cap, token_mean),
        out_shape=(
            jax.ShapeDtypeStruct((rows, half), b16),
            jax.ShapeDtypeStruct((rank, chunk), f32),
            jax.ShapeDtypeStruct((rank, hidden), f32),
            jax.ShapeDtypeStruct((rank, chunk), f32),
            jax.ShapeDtypeStruct((8, chunk), f32),
        ),
        in_specs=[hbm, vmem, vmem, hbm, hbm, hbm],
        out_specs=(vmem,) * 5,
        scratch_shapes=[
            pltpu.VMEM((rows, width), b16),
            pltpu.VMEM((rank, width), b16),
            pltpu.VMEM((width, hidden), b16),
            pltpu.VMEM((chunk, hidden), f32),
            pltpu.VMEM((chunk, hidden), b16),
            pltpu.VMEM((chunk, hidden), b16),
            pltpu.VMEM((n_exp - 1, cap, width), b16),
            pltpu.VMEM((n_exp, cap, width), b16),
            pltpu.VMEM((n_exp, 2, cap, half), b16),
            pltpu.VMEM((n_exp, 2, cap, half), b16),
            pltpu.VMEM((n_dp, rank + 8, chunk), f32),
            pltpu.VMEM((n_dp, rank + 8, chunk), f32),
            pltpu.VMEM((rank, 2 * rank), f32),
            pltpu.VMEM((n_dp, rank, 2 * rank), f32),
            pltpu.VMEM((rank, hidden), f32),
            pltpu.VMEM((n_dp, rank, hidden), f32),
            pltpu.VMEM((rank, 2 * rank), f32),
            dma((4,)), dma((n_exp,)), dma((n_exp,)), dma((n_exp, 2)), dma((n_exp, 2)),
            dma((n_dp,)), dma((n_dp,)), dma((n_dp,)), dma((n_dp,)), dma((n_dp,)), dma((n_dp,)),
        ],
        compiler_params=pltpu.CompilerParams(
            collective_id=0, has_side_effects=True, vmem_limit_bytes=48 * 1024 * 1024
        ),
    )(tokens, routing.T, gate_values.T, expert_weight[0], subspace[0], gradient[0, 0])
    block = 128
    result = pl.pallas_call(
        finish_block,
        grid=(chunk // block,),
        out_shape=jax.ShapeDtypeStruct((chunk, hidden), f32),
        in_specs=[
            pl.BlockSpec((block, hidden), lambda i: (i, 0)),
            pl.BlockSpec((rank, block), lambda i: (0, i)),
            pl.BlockSpec((8, block), lambda i: (0, i)),
            pl.BlockSpec((rank, hidden), lambda i: (0, 0)),
        ],
        out_specs=pl.BlockSpec((block, hidden), lambda i: (i, 0)),
        scratch_shapes=[pltpu.VMEM((4 * rank, hidden), b16)],
    )(gradient[0, 0], scaled, recip, solved)
    return (combined, basis[None, None], result[None, None])


def solution(mesh):
    in_specs = (
        P(("dp", "expert"), "tensor"),
        P(("dp", "expert"), None),
        P(("dp", "expert"), None),
        P("expert", "tensor", None),
        P("expert", None, "tensor"),
        P("expert", "tensor", "dp", None),
    )
    out_specs = (
        P(("dp", "expert"), "tensor"),
        P("expert", "tensor", None, "dp"),
        P("expert", "tensor", "dp", None),
    )

    def run(tokens, routing, gate_values, expert_weight, subspace, gradient):
        sizes = dict(mesh.shape)
        if fits(sizes, tokens, subspace, gradient, expert_weight):
            return fast(sizes, tokens, routing, gate_values, expert_weight, subspace, gradient)
        return body(tokens, routing, gate_values, expert_weight, subspace, gradient)

    return jax.shard_map(run, mesh=mesh, in_specs=in_specs, out_specs=out_specs, check_vma=False)
```

```python
import functools

import jax
import jax.numpy as jnp
from jax import lax
from jax.experimental import pallas as pl
from jax.experimental.pallas import tpu as pltpu
from jax.sharding import PartitionSpec as P

EPSILON = 1e-05


def tri_solve(factor, rhs, flip):
    return lax.linalg.triangular_solve(factor, rhs, left_side=True, lower=True, transpose_a=flip)


def finish(image_mine, diagonal, grad_rows, gram_matrix, curvature, inner_term, token_mean):
    highest = lax.Precision.HIGHEST
    factor_low = jnp.linalg.cholesky(gram_matrix)
    eigen_scale = jnp.diagonal(factor_low) / token_mean
    middle = jnp.dot(factor_low / eigen_scale[None, :], factor_low.T, precision=highest) + curvature
    factor_mid = jnp.linalg.cholesky(middle)
    solved = tri_solve(factor_mid, tri_solve(factor_mid, inner_term, False), True)
    scaled = image_mine / diagonal[None, :]
    result = grad_rows / diagonal[:, None] - jnp.dot(scaled.T, solved, precision=highest)
    basis_out = tri_solve(factor_low, image_mine, False)
    return (basis_out, result)


def body(tokens, routing, gate_values, expert_weight, subspace, gradient):
    highest = lax.Precision.HIGHEST
    tok_rows, half_width = tokens.shape
    choose_count = routing.shape[1]
    owners = lax.axis_size("expert")
    tensor_count = lax.axis_size("tensor")
    capacity = tok_rows * choose_count // owners * 9 // 8
    pair_count = tok_rows * choose_count
    slot_count = owners * capacity
    hidden_units = expert_weight.shape[2]
    flat_ids = routing.reshape(pair_count)
    one_hot = (flat_ids[:, None] == jnp.arange(owners, dtype=jnp.int32)[None, :]).astype(
        jnp.float32
    )
    pair_index = jnp.arange(pair_count, dtype=jnp.int32)
    strict_lower = (pair_index[:, None] > pair_index[None, :]).astype(jnp.float32)
    before = jnp.dot(strict_lower, one_hot, preferred_element_type=jnp.float32)
    position = jnp.sum(before * one_hot, axis=1).astype(jnp.int32)
    slot_ids = flat_ids * capacity + position
    matches = (jnp.arange(slot_count, dtype=jnp.int32)[:, None] == slot_ids[None, :]).reshape(
        slot_count, tok_rows, choose_count
    )
    picker = jnp.sum(matches.astype(jnp.float32), axis=2).astype(jnp.bfloat16)
    outgoing = jnp.dot(picker, tokens, preferred_element_type=jnp.float32).astype(jnp.bfloat16)
    outgoing = outgoing.reshape(owners, capacity, half_width)
    incoming = lax.all_to_all(outgoing, "expert", split_axis=0, concat_axis=0, tiled=True)
    slab_rows = incoming.reshape(slot_count, half_width)
    partial_value = jnp.dot(slab_rows, expert_weight[0], preferred_element_type=jnp.float32).astype(
        jnp.bfloat16
    )
    shaped = partial_value.reshape(owners, capacity, tensor_count, hidden_units // tensor_count)
    returned = lax.all_to_all(
        lax.all_to_all(shaped, "expert", split_axis=0, concat_axis=0, tiled=True),
        "tensor",
        split_axis=2,
        concat_axis=2,
        tiled=True,
    )
    hidden = jnp.sum(returned.astype(jnp.float32), axis=2).reshape(
        slot_count, hidden_units // tensor_count
    )
    weighting = jnp.sum(matches.astype(jnp.float32) * gate_values[None, :, :], axis=2).T
    combined = jnp.dot(weighting, hidden, precision=highest).astype(jnp.bfloat16)
    projected = lax.dot_general(
        slab_rows, subspace[0], (((1,), (1,)), ((), ())), preferred_element_type=jnp.float32
    ).astype(jnp.bfloat16)
    image_rows = lax.dot_general(
        projected, slab_rows, (((0,), (0,)), ((), ())), preferred_element_type=jnp.float32
    )
    square_sums = jnp.sum(jnp.square(slab_rows.astype(jnp.float32)), axis=0)
    stacked = jnp.concatenate([image_rows, square_sums[None, :]], axis=0)
    rank_rows = image_rows.shape[0]
    token_mean = float(tok_rows * choose_count * lax.axis_size("dp"))
    grad_rows = gradient[0, 0]
    summed = lax.psum_scatter(stacked, "dp", scatter_dimension=1, tiled=True)
    image_mine = summed[:rank_rows]
    diagonal = summed[rank_rows] / token_mean + EPSILON
    scaled = image_mine / diagonal[None, :]
    gram_part = jnp.dot(image_mine, image_mine.T, precision=highest)
    curve_part = jnp.dot(scaled, image_mine.T, precision=highest)
    inner_part = jnp.dot(scaled, grad_rows, precision=highest)
    gram_matrix, curvature, inner_term = lax.psum((gram_part, curve_part, inner_part), "dp")
    basis_out, result = finish(
        image_mine, diagonal, grad_rows, gram_matrix, curvature, inner_term, token_mean
    )
    return (combined, basis_out[None, None], result[None, None])


HIGHEST = lax.Precision.HIGHEST
MESH = pl.DeviceIdType.MESH


def is_power(n):
    return n & (n - 1) == 0


def fits(sizes, tokens, subspace, gradient, expert_weight):
    few = sizes["dp"] == 4 and sizes["expert"] <= 4 and sizes["tensor"] == 2
    even = is_power(sizes["expert"])
    lanes = gradient.shape[2] % 128 == 0 and expert_weight.shape[2] % 256 == 0
    return few and even and lanes and subspace.shape[1] == 64 and tokens.shape[0] == 128


def flip(index, k, n):
    out, bit = 0, 1
    while bit < n:
        own = lax.rem(index // bit, 2)
        out = out + bit * (1 - own if (k // bit) % 2 else own)
        bit *= 2
    return out


def split(x):
    high = x.astype(jnp.bfloat16)
    low = (x - high.astype(jnp.float32)).astype(jnp.bfloat16)
    return high, low


def f32_dot(a, b, dims):
    return lax.dot_general(a, b, (dims, ((), ())), preferred_element_type=jnp.float32)


def eliminate(matrix):
    rank = matrix.shape[0]
    row_id = lax.broadcasted_iota(jnp.int32, (rank, 2 * rank), 0)
    eye = (lax.broadcasted_iota(jnp.int32, (rank, rank), 0) == lax.broadcasted_iota(jnp.int32, (rank, rank), 1)).astype(jnp.float32)
    state = jnp.concatenate([matrix, eye], axis=1)
    group = 8
    for j in range(0, rank, group):
        cols = [jnp.broadcast_to(state[:, j + i:j + i + 1], (rank, 2 * rank)) for i in range(group)]
        rows = [state[j + i:j + i + 1, :] for i in range(group)]
        delta = None
        for i in range(group):
            inverse = 1.0 / cols[i][j + i:j + i + 1, :]
            factor = jnp.where(row_id > j + i, cols[i] * inverse, 0.0)
            for m in range(i + 1, group):
                ratio = cols[i][j + m:j + m + 1, :] * inverse
                rows[m] = rows[m] - ratio * rows[i]
                cols[m] = cols[m] - cols[i] * ratio
            term = factor * rows[i]
            delta = term if delta is None else delta + term
        state = state - delta
    return state[:, :rank], state[:, rank:], jnp.sum(state[:, :rank] * eye, axis=1, keepdims=True)


def exchange(n_dp, n_exp, cap, token_mean, tok_hbm, route_hbm, gate_hbm, w_hbm, sub_hbm, grad_hbm,
             comb_hbm, basis_hbm, result_hbm,
             tok, route_ref, gate_ref, sub, wgt, grad, g_high, g_low, out_rows, in_rows, parts, ret, image, forward, rs_in,
             small, small_in, inner, inner_mid, inner_in, left, comb, basis,
             loc_sem, out_sem, tok_s, tok_r, ret_s, ret_r, rs_s, rs_r, sm_s, sm_r, in_s, in_r):
    dp = lax.axis_index("dp")
    ex = lax.axis_index("expert")
    core = lax.axis_index("tensor")
    half = parts.shape[3]
    width = tok.shape[1]
    chunk = width // n_dp
    rank = sub.shape[0]
    rows = tok.shape[0]
    cut = (rank + 8) // 16 * 8 + 8 * ((rank + 8) // 8 % 2)

    loads = [
        pltpu.make_async_copy(tok_hbm, tok, loc_sem.at[0]),
        pltpu.make_async_copy(sub_hbm, sub, loc_sem.at[1]),
        pltpu.make_async_copy(w_hbm, wgt, loc_sem.at[2]),
        pltpu.make_async_copy(grad_hbm, grad, loc_sem.at[3]),
        pltpu.make_async_copy(route_hbm, route_ref, loc_sem.at[4]),
        pltpu.make_async_copy(gate_hbm, gate_ref, loc_sem.at[5]),
    ]
    for i in (4, 0, 1, 5, 2, 3):
        loads[i].start()

    barrier = pltpu.get_barrier_semaphore()
    peers = [(dp, flip(ex, k, n_exp), core) for k in range(1, n_exp)]
    peers += [(dp, flip(ex, k, n_exp), 1 - core) for k in range(n_exp)]
    peers += [(flip(dp, k, n_dp), ex, core) for k in range(1, n_dp)]
    for peer in peers:
        pl.semaphore_signal(barrier, inc=1, device_id=peer, device_id_type=MESH)

    row_i = lax.broadcasted_iota(jnp.int32, (rows, rows), 0)
    col_i = lax.broadcasted_iota(jnp.int32, (rows, rows), 1)
    earlier = (row_i < col_i).astype(jnp.float32)
    slot_i = lax.broadcasted_iota(jnp.int32, (cap, rows), 0)
    loads[4].wait()
    named = []
    for k in range(n_exp):
        hit = route_ref[...] == flip(ex, k, n_exp)
        named.append(jnp.sum(hit.astype(jnp.float32), axis=0, keepdims=True))
    named8 = jnp.concatenate(named + [jnp.zeros((8 - n_exp, rows), jnp.float32)], axis=0)
    before = f32_dot(named8.astype(jnp.bfloat16), earlier.astype(jnp.bfloat16), ((1,), (0,)))

    def picker(k):
        place = before[k:k + 1].astype(jnp.int32)
        return jnp.where((slot_i == place) & (named8[k:k + 1] > 0.5), 1.0, 0.0).astype(jnp.bfloat16)

    pickers = [picker(k) for k in range(n_exp)]
    loads[0].wait()
    pl.semaphore_wait(barrier, len(peers))

    sends = []

    def send(src, dst, s, r, peer):
        copy = pltpu.make_async_remote_copy(
            src_ref=src, dst_ref=dst, send_sem=s, recv_sem=r, device_id=peer, device_id_type=MESH
        )
        copy.start()
        return copy

    tok_copies = {}
    for k in list(range(n_exp - 1, 0, -1)):
        out_rows[k - 1] = f32_dot(pickers[k], tok[...], ((1,), (0,))).astype(jnp.bfloat16)
        tok_copies[k] = send(out_rows.at[k - 1], in_rows.at[k], tok_s.at[k], tok_r.at[k], (dp, flip(ex, k, n_exp), core))
    in_rows[0] = f32_dot(pickers[0], tok[...], ((1,), (0,))).astype(jnp.bfloat16)
    loads[1].wait()

    def add_image(k):
        got = in_rows.at[k]
        projected = f32_dot(got[...], sub[...], ((1,), (1,))).astype(jnp.bfloat16)
        for j in range(n_dp):
            part = got[:, j * chunk:(j + 1) * chunk]
            img = f32_dot(projected, part, ((0,), (0,)))
            wide = part.astype(jnp.float32)
            sq = jnp.sum(wide * wide, axis=0, keepdims=True)
            if k == 0:
                image[j, :rank] = img
                image[j, rank:rank + 8] = jnp.broadcast_to(sq, (8, chunk))
            else:
                image[j, :rank] += img
                image[j, rank:rank + 8] += jnp.broadcast_to(sq, (8, chunk))

    ret_copies = {}

    def project(k):
        for rel in range(2):
            which = core if rel == 0 else 1 - core
            cols = pl.ds(pl.multiple_of(which * half, half), half)
            value = f32_dot(in_rows[k], wgt[:, cols], ((1,), (0,))).astype(jnp.bfloat16)
            if k == 0 and rel == 0:
                ret[0, 0] = value
            else:
                parts[k, rel] = value
                peer = (dp, flip(ex, k, n_exp), which)
                ret_copies[k, rel] = send(parts.at[k, rel], ret.at[k, rel], ret_s.at[k, rel], ret_r.at[k, rel], peer)

    add_image(0)
    loads[2].wait()
    project(0)
    loads[3].wait()
    high, low = split(grad[...])
    g_high[...] = high
    g_low[...] = low
    order = list(range(1, n_exp))
    for k in order:
        tok_copies[k].wait_recv()
        add_image(k)
        if k != order[-1]:
            project(k)

    bounds = ((0, cut), (cut, rank + 8))
    firsts = (1, 2)
    rs_copies = {}
    for turn in (0, 1):
        for part in range(2):
            lo, hi = bounds[part]
            near = firsts[part]
            to = flip(dp, near, n_dp)
            which = flip(dp, 3, n_dp) if turn == 0 else to
            rs_copies[part, turn] = send(
                image.at[which, lo:hi], rs_in.at[turn, lo:hi], rs_s.at[part, turn], rs_r.at[part, turn], (to, ex, core)
            )
    project(order[-1])
    for part in range(2):
        lo, hi = bounds[part]
        far = 3 - firsts[part]
        to = flip(dp, far, n_dp)
        rs_copies[part, 0].wait_recv()
        forward[lo:hi] = image[to, lo:hi] + rs_in[0, lo:hi]
        rs_copies[part, 2] = send(
            forward.at[lo:hi], rs_in.at[2, lo:hi], rs_s.at[part, 2], rs_r.at[part, 2], (to, ex, core)
        )
    for turn in (1, 2):
        for part in range(2):
            rs_copies[part, turn].wait_recv()
    total = image[dp] + rs_in[1] + rs_in[2]
    mine = total[:rank]
    recip = 1.0 / (total[rank:rank + 1] / token_mean + EPSILON)
    scaled = mine * recip
    both = jnp.concatenate([mine, scaled], axis=0)
    small[...] = lax.dot_general(mine, both, (((1,), (1,)), ((), ())), precision=HIGHEST, preferred_element_type=jnp.float32)
    sm_copies = {}
    for k in range(n_dp - 1, 0, -1):
        sm_copies[k] = send(small, small_in.at[k], sm_s.at[k], sm_r.at[k], (flip(dp, k, n_dp), ex, core))
    s_high, s_low = split(scaled)
    s_both = jnp.concatenate([s_high, s_low], axis=0)
    cross = f32_dot(s_both, g_high[...], ((1,), (0,)))
    inner[...] = cross[:rank] + cross[rank:] + f32_dot(s_high, g_low[...], ((1,), (0,)))
    in_copies = {}
    mid = rank // 2
    for part in range(2):
        rows_of = slice(part * mid, part * mid + mid)
        in_copies[part, 0] = send(
            inner.at[rows_of], inner_in.at[0, rows_of], in_s.at[part, 0], in_r.at[part, 0], (flip(dp, firsts[part], n_dp), ex, core)
        )
    left[...] = jnp.concatenate([s_high, s_high, s_low, s_low], axis=0).T
    recip_cols = jnp.broadcast_to(recip, (8, chunk)).T
    for c in range(0, chunk, 128):
        grad[c:c + 128] = grad[c:c + 128] * recip_cols[c:c + 128, :1]

    sums = small[...]
    for k in range(1, n_dp):
        sm_copies[k].wait_recv()
        sums = sums + small_in[k]
    upper, lower_inv, pivots = eliminate(sums[:, :rank])
    for part in range(2):
        rows_of = slice(part * mid, part * mid + mid)
        in_copies[part, 0].wait_recv()
        inner_mid[rows_of] = inner[rows_of] + inner_in[0, rows_of]
        in_copies[part, 1] = send(
            inner_mid.at[rows_of], inner_in.at[1, rows_of], in_s.at[part, 1], in_r.at[part, 1], (flip(dp, 3 - firsts[part], n_dp), ex, core)
        )
    root = lax.rsqrt(pivots)
    transposed = upper * root
    middle = lax.dot_general(transposed * (root * token_mean), transposed, (((0,), (0,)), ((), ())), precision=HIGHEST, preferred_element_type=jnp.float32)
    middle = middle + sums[:, rank:]
    _, mid_inv, mid_pivots = eliminate(middle)
    inverse = lax.dot_general(mid_inv / mid_pivots, mid_inv, (((0,), (0,)), ((), ())), precision=HIGHEST, preferred_element_type=jnp.float32)
    basis[...] = root * lax.dot_general(lower_inv, mine, (((1,), (0,)), ((), ())), precision=HIGHEST, preferred_element_type=jnp.float32)
    stores = [pltpu.make_async_copy(basis, basis_hbm, out_sem.at[0])]
    stores[0].start()

    loads[5].wait()
    gates = []
    for k in range(n_exp):
        hit = (route_ref[...] == flip(ex, k, n_exp)).astype(jnp.float32)
        gates.append(jnp.sum(hit * gate_ref[...], axis=0, keepdims=True))
    gates8 = jnp.concatenate(gates + [jnp.zeros((8 - n_exp, rows), jnp.float32)], axis=0)
    gate_cols = gates8.T
    combined = jnp.zeros((rows, half), jnp.float32)
    for k in range(n_exp):
        hidden = jnp.zeros((rows, half), jnp.float32)
        for rel in range(2):
            if (k, rel) in ret_copies:
                ret_copies[k, rel].wait_recv()
            hidden = hidden + f32_dot(pickers[k], ret[k, rel], ((0,), (0,)))
        combined = combined + gate_cols[:, k:k + 1] * hidden
    comb[...] = combined.astype(jnp.bfloat16)
    stores.append(pltpu.make_async_copy(comb, comb_hbm, out_sem.at[1]))
    stores[1].start()

    for part in range(2):
        in_copies[part, 1].wait_recv()
    inner_sum = inner_mid[...] + inner_in[1]
    solved = lax.dot_general(inverse, inner_sum, (((1,), (0,)), ((), ())), precision=HIGHEST, preferred_element_type=jnp.float32)
    v_high, v_low = split(solved)
    right = jnp.concatenate([v_high, v_low, v_high, v_low], axis=0)
    for c in range(0, chunk, 128):
        grad[c:c + 128] = grad[c:c + 128] - f32_dot(left[c:c + 128], right, ((1,), (0,)))
        store = pltpu.make_async_copy(grad.at[c:c + 128], result_hbm.at[c:c + 128], out_sem.at[2 + c // 128])
        store.start()
        stores.append(store)

    for group in (tok_copies, ret_copies, rs_copies, sm_copies, in_copies):
        for copy in group.values():
            copy.wait_send()
    for store in stores:
        store.wait()


def fast(sizes, tokens, routing, gate_values, expert_weight, subspace, gradient):
    n_dp, n_exp = sizes["dp"], sizes["expert"]
    rows, width = tokens.shape
    choices = routing.shape[1]
    cap = rows * choices // n_exp * 9 // 8
    cap = -(-cap // 8) * 8
    rank = subspace.shape[1]
    hidden = expert_weight.shape[2]
    half = hidden // 2
    chunk = width // n_dp
    token_mean = float(rows * choices * n_dp)
    f32, b16 = jnp.float32, jnp.bfloat16
    hbm = pl.BlockSpec(memory_space=pl.ANY)
    vmem = pl.BlockSpec(memory_space=pltpu.VMEM)
    dma = pltpu.SemaphoreType.DMA
    combined, basis, result = pl.pallas_call(
        functools.partial(exchange, n_dp, n_exp, cap, token_mean),
        out_shape=(
            jax.ShapeDtypeStruct((rows, half), b16),
            jax.ShapeDtypeStruct((rank, chunk), f32),
            jax.ShapeDtypeStruct((chunk, hidden), f32),
        ),
        in_specs=[hbm] * 6,
        out_specs=(hbm,) * 3,
        scratch_shapes=[
            pltpu.VMEM((rows, width), b16),
            pltpu.VMEM((choices, rows), jnp.int32),
            pltpu.VMEM((choices, rows), f32),
            pltpu.VMEM((rank, width), b16),
            pltpu.VMEM((width, hidden), b16),
            pltpu.VMEM((chunk, hidden), f32),
            pltpu.VMEM((chunk, hidden), b16),
            pltpu.VMEM((chunk, hidden), b16),
            pltpu.VMEM((n_exp - 1, cap, width), b16),
            pltpu.VMEM((n_exp, cap, width), b16),
            pltpu.VMEM((n_exp, 2, cap, half), b16),
            pltpu.VMEM((n_exp, 2, cap, half), b16),
            pltpu.VMEM((n_dp, rank + 8, chunk), f32),
            pltpu.VMEM((rank + 8, chunk), f32),
            pltpu.VMEM((3, rank + 8, chunk), f32),
            pltpu.VMEM((rank, 2 * rank), f32),
            pltpu.VMEM((n_dp, rank, 2 * rank), f32),
            pltpu.VMEM((rank, hidden), f32),
            pltpu.VMEM((rank, hidden), f32),
            pltpu.VMEM((2, rank, hidden), f32),
            pltpu.VMEM((chunk, 4 * rank), b16),
            pltpu.VMEM((rows, half), b16),
            pltpu.VMEM((rank, chunk), f32),
            dma((6,)), dma((2 + chunk // 128,)), dma((n_exp,)), dma((n_exp,)), dma((n_exp, 2)), dma((n_exp, 2)),
            dma((2, 3)), dma((2, 3)), dma((n_dp,)), dma((n_dp,)), dma((2, 2)), dma((2, 2)),
        ],
        compiler_params=pltpu.CompilerParams(
            collective_id=0, has_side_effects=True, vmem_limit_bytes=67000000
        ),
    )(tokens, routing.T, gate_values.T, expert_weight[0], subspace[0], gradient[0, 0])
    return (combined, basis[None, None], result[None, None])


def solution(mesh):
    in_specs = (
        P(("dp", "expert"), "tensor"),
        P(("dp", "expert"), None),
        P(("dp", "expert"), None),
        P("expert", "tensor", None),
        P("expert", None, "tensor"),
        P("expert", "tensor", "dp", None),
    )
    out_specs = (
        P(("dp", "expert"), "tensor"),
        P("expert", "tensor", None, "dp"),
        P("expert", "tensor", "dp", None),
    )

    def run(tokens, routing, gate_values, expert_weight, subspace, gradient):
        sizes = dict(mesh.shape)
        if fits(sizes, tokens, subspace, gradient, expert_weight):
            return fast(sizes, tokens, routing, gate_values, expert_weight, subspace, gradient)
        return body(tokens, routing, gate_values, expert_weight, subspace, gradient)

    return jax.shard_map(run, mesh=mesh, in_specs=in_specs, out_specs=out_specs, check_vma=False)
```

```python
import functools

import jax
import jax.numpy as jnp
from jax import lax
from jax.experimental import pallas as pl
from jax.experimental.pallas import tpu as pltpu
from jax.sharding import PartitionSpec as P

EPSILON = 1e-05


def tri_solve(factor, rhs, flip):
    return lax.linalg.triangular_solve(factor, rhs, left_side=True, lower=True, transpose_a=flip)


def finish(image_mine, diagonal, grad_rows, gram_matrix, curvature, inner_term, token_mean):
    highest = lax.Precision.HIGHEST
    factor_low = jnp.linalg.cholesky(gram_matrix)
    eigen_scale = jnp.diagonal(factor_low) / token_mean
    middle = jnp.dot(factor_low / eigen_scale[None, :], factor_low.T, precision=highest) + curvature
    factor_mid = jnp.linalg.cholesky(middle)
    solved = tri_solve(factor_mid, tri_solve(factor_mid, inner_term, False), True)
    scaled = image_mine / diagonal[None, :]
    result = grad_rows / diagonal[:, None] - jnp.dot(scaled.T, solved, precision=highest)
    basis_out = tri_solve(factor_low, image_mine, False)
    return (basis_out, result)


def body(tokens, routing, gate_values, expert_weight, subspace, gradient):
    highest = lax.Precision.HIGHEST
    tok_rows, half_width = tokens.shape
    choose_count = routing.shape[1]
    owners = lax.axis_size("expert")
    tensor_count = lax.axis_size("tensor")
    capacity = tok_rows * choose_count // owners * 9 // 8
    pair_count = tok_rows * choose_count
    slot_count = owners * capacity
    hidden_units = expert_weight.shape[2]
    flat_ids = routing.reshape(pair_count)
    one_hot = (flat_ids[:, None] == jnp.arange(owners, dtype=jnp.int32)[None, :]).astype(
        jnp.float32
    )
    pair_index = jnp.arange(pair_count, dtype=jnp.int32)
    strict_lower = (pair_index[:, None] > pair_index[None, :]).astype(jnp.float32)
    before = jnp.dot(strict_lower, one_hot, preferred_element_type=jnp.float32)
    position = jnp.sum(before * one_hot, axis=1).astype(jnp.int32)
    slot_ids = flat_ids * capacity + position
    matches = (jnp.arange(slot_count, dtype=jnp.int32)[:, None] == slot_ids[None, :]).reshape(
        slot_count, tok_rows, choose_count
    )
    picker = jnp.sum(matches.astype(jnp.float32), axis=2).astype(jnp.bfloat16)
    outgoing = jnp.dot(picker, tokens, preferred_element_type=jnp.float32).astype(jnp.bfloat16)
    outgoing = outgoing.reshape(owners, capacity, half_width)
    incoming = lax.all_to_all(outgoing, "expert", split_axis=0, concat_axis=0, tiled=True)
    slab_rows = incoming.reshape(slot_count, half_width)
    partial_value = jnp.dot(slab_rows, expert_weight[0], preferred_element_type=jnp.float32).astype(
        jnp.bfloat16
    )
    shaped = partial_value.reshape(owners, capacity, tensor_count, hidden_units // tensor_count)
    returned = lax.all_to_all(
        lax.all_to_all(shaped, "expert", split_axis=0, concat_axis=0, tiled=True),
        "tensor",
        split_axis=2,
        concat_axis=2,
        tiled=True,
    )
    hidden = jnp.sum(returned.astype(jnp.float32), axis=2).reshape(
        slot_count, hidden_units // tensor_count
    )
    weighting = jnp.sum(matches.astype(jnp.float32) * gate_values[None, :, :], axis=2).T
    combined = jnp.dot(weighting, hidden, precision=highest).astype(jnp.bfloat16)
    projected = lax.dot_general(
        slab_rows, subspace[0], (((1,), (1,)), ((), ())), preferred_element_type=jnp.float32
    ).astype(jnp.bfloat16)
    image_rows = lax.dot_general(
        projected, slab_rows, (((0,), (0,)), ((), ())), preferred_element_type=jnp.float32
    )
    square_sums = jnp.sum(jnp.square(slab_rows.astype(jnp.float32)), axis=0)
    stacked = jnp.concatenate([image_rows, square_sums[None, :]], axis=0)
    rank_rows = image_rows.shape[0]
    token_mean = float(tok_rows * choose_count * lax.axis_size("dp"))
    grad_rows = gradient[0, 0]
    summed = lax.psum_scatter(stacked, "dp", scatter_dimension=1, tiled=True)
    image_mine = summed[:rank_rows]
    diagonal = summed[rank_rows] / token_mean + EPSILON
    scaled = image_mine / diagonal[None, :]
    gram_part = jnp.dot(image_mine, image_mine.T, precision=highest)
    curve_part = jnp.dot(scaled, image_mine.T, precision=highest)
    inner_part = jnp.dot(scaled, grad_rows, precision=highest)
    gram_matrix, curvature, inner_term = lax.psum((gram_part, curve_part, inner_part), "dp")
    basis_out, result = finish(
        image_mine, diagonal, grad_rows, gram_matrix, curvature, inner_term, token_mean
    )
    return (combined, basis_out[None, None], result[None, None])


HIGHEST = lax.Precision.HIGHEST
MESH = pl.DeviceIdType.MESH


def is_power(n):
    return n & (n - 1) == 0


def fits(sizes, tokens, subspace, gradient, expert_weight):
    few = sizes["dp"] == 4 and sizes["expert"] <= 4 and sizes["tensor"] == 2
    even = is_power(sizes["expert"])
    lanes = gradient.shape[2] % 128 == 0 and expert_weight.shape[2] % 256 == 0
    return few and even and lanes and subspace.shape[1] == 64 and tokens.shape[0] == 128


def flip(index, k, n):
    out, bit = 0, 1
    while bit < n:
        own = lax.rem(index // bit, 2)
        out = out + bit * (1 - own if (k // bit) % 2 else own)
        bit *= 2
    return out


def split(x):
    high = x.astype(jnp.bfloat16)
    low = (x - high.astype(jnp.float32)).astype(jnp.bfloat16)
    return high, low


def f32_dot(a, b, dims):
    return lax.dot_general(a, b, (dims, ((), ())), preferred_element_type=jnp.float32)


def eliminate(matrix):
    rank = matrix.shape[0]
    row_id = lax.broadcasted_iota(jnp.int32, (rank, 2 * rank), 0)
    eye = (lax.broadcasted_iota(jnp.int32, (rank, rank), 0) == lax.broadcasted_iota(jnp.int32, (rank, rank), 1)).astype(jnp.float32)
    state = jnp.concatenate([matrix, eye], axis=1)
    group = 8
    for j in range(0, rank, group):
        cols = [jnp.broadcast_to(state[:, j + i:j + i + 1], (rank, 2 * rank)) for i in range(group)]
        rows = [state[j + i:j + i + 1, :] for i in range(group)]
        delta = None
        for i in range(group):
            inverse = 1.0 / cols[i][j + i:j + i + 1, :]
            factor = jnp.where(row_id > j + i, cols[i] * inverse, 0.0)
            for m in range(i + 1, group):
                ratio = cols[i][j + m:j + m + 1, :] * inverse
                rows[m] = rows[m] - ratio * rows[i]
                cols[m] = cols[m] - cols[i] * ratio
            term = factor * rows[i]
            delta = term if delta is None else delta + term
        state = state - delta
    return state[:, :rank], state[:, rank:], jnp.sum(state[:, :rank] * eye, axis=1, keepdims=True)


def exchange(n_dp, n_exp, cap, token_mean, tok_hbm, route_hbm, gate_hbm, w_hbm, sub_hbm, grad_hbm,
             comb_hbm, basis_hbm, left_hbm, recip_hbm, solved_hbm,
             tok, route_ref, gate_ref, sub, wgt, grad, g_high, g_low, out_rows, in_rows, parts, ret, image, forward, rs_in,
             small, small_in, inner, inner_mid, inner_in, left, comb, basis, recips, solved,
             loc_sem, out_sem, tok_s, tok_r, ret_s, ret_r, rs_s, rs_r, sm_s, sm_r, in_s, in_r):
    dp = lax.axis_index("dp")
    ex = lax.axis_index("expert")
    core = lax.axis_index("tensor")
    half = parts.shape[3]
    width = tok.shape[1]
    chunk = width // n_dp
    rank = sub.shape[0]
    rows = tok.shape[0]
    cut = (rank + 8) // 16 * 8 + 8 * ((rank + 8) // 8 % 2)

    loads = [
        pltpu.make_async_copy(tok_hbm, tok, loc_sem.at[0]),
        pltpu.make_async_copy(sub_hbm, sub, loc_sem.at[1]),
        pltpu.make_async_copy(w_hbm, wgt, loc_sem.at[2]),
        pltpu.make_async_copy(grad_hbm, grad, loc_sem.at[3]),
        pltpu.make_async_copy(route_hbm, route_ref, loc_sem.at[4]),
        pltpu.make_async_copy(gate_hbm, gate_ref, loc_sem.at[5]),
    ]
    for i in (4, 0, 1, 5, 2, 3):
        loads[i].start()

    barrier = pltpu.get_barrier_semaphore()
    peers = [(dp, flip(ex, k, n_exp), core) for k in range(1, n_exp)]
    peers += [(dp, flip(ex, k, n_exp), 1 - core) for k in range(n_exp)]
    peers += [(flip(dp, k, n_dp), ex, core) for k in range(1, n_dp)]
    for peer in peers:
        pl.semaphore_signal(barrier, inc=1, device_id=peer, device_id_type=MESH)

    row_i = lax.broadcasted_iota(jnp.int32, (rows, rows), 0)
    col_i = lax.broadcasted_iota(jnp.int32, (rows, rows), 1)
    earlier = (row_i < col_i).astype(jnp.float32)
    slot_i = lax.broadcasted_iota(jnp.int32, (cap, rows), 0)
    loads[4].wait()
    named = []
    for k in range(n_exp):
        hit = route_ref[...] == flip(ex, k, n_exp)
        named.append(jnp.sum(hit.astype(jnp.float32), axis=0, keepdims=True))
    named8 = jnp.concatenate(named + [jnp.zeros((8 - n_exp, rows), jnp.float32)], axis=0)
    before = f32_dot(named8.astype(jnp.bfloat16), earlier.astype(jnp.bfloat16), ((1,), (0,)))

    def picker(k):
        place = before[k:k + 1].astype(jnp.int32)
        return jnp.where((slot_i == place) & (named8[k:k + 1] > 0.5), 1.0, 0.0).astype(jnp.bfloat16)

    pickers = [picker(k) for k in range(n_exp)]
    loads[0].wait()
    pl.semaphore_wait(barrier, len(peers))

    sends = []

    def send(src, dst, s, r, peer):
        copy = pltpu.make_async_remote_copy(
            src_ref=src, dst_ref=dst, send_sem=s, recv_sem=r, device_id=peer, device_id_type=MESH
        )
        copy.start()
        return copy

    tok_copies = {}
    for k in list(range(n_exp - 1, 0, -1)):
        out_rows[k - 1] = f32_dot(pickers[k], tok[...], ((1,), (0,))).astype(jnp.bfloat16)
        tok_copies[k] = send(out_rows.at[k - 1], in_rows.at[k], tok_s.at[k], tok_r.at[k], (dp, flip(ex, k, n_exp), core))
    in_rows[0] = f32_dot(pickers[0], tok[...], ((1,), (0,))).astype(jnp.bfloat16)
    loads[1].wait()

    def add_image(k):
        got = in_rows.at[k]
        projected = f32_dot(got[...], sub[...], ((1,), (1,))).astype(jnp.bfloat16)
        for j in range(n_dp):
            part = got[:, j * chunk:(j + 1) * chunk]
            img = f32_dot(projected, part, ((0,), (0,)))
            wide = part.astype(jnp.float32)
            sq = jnp.sum(wide * wide, axis=0, keepdims=True)
            if k == 0:
                image[j, :rank] = img
                image[j, rank:rank + 8] = jnp.broadcast_to(sq, (8, chunk))
            else:
                image[j, :rank] += img
                image[j, rank:rank + 8] += jnp.broadcast_to(sq, (8, chunk))

    ret_copies = {}

    def project(k):
        for rel in range(2):
            which = core if rel == 0 else 1 - core
            cols = pl.ds(pl.multiple_of(which * half, half), half)
            value = f32_dot(in_rows[k], wgt[:, cols], ((1,), (0,))).astype(jnp.bfloat16)
            if k == 0 and rel == 0:
                ret[0, 0] = value
            else:
                parts[k, rel] = value
                peer = (dp, flip(ex, k, n_exp), which)
                ret_copies[k, rel] = send(parts.at[k, rel], ret.at[k, rel], ret_s.at[k, rel], ret_r.at[k, rel], peer)

    add_image(0)
    loads[2].wait()
    project(0)
    loads[3].wait()
    high, low = split(grad[...])
    g_high[...] = high
    g_low[...] = low
    order = list(range(1, n_exp))
    for k in order:
        tok_copies[k].wait_recv()
        add_image(k)
        if k != order[-1]:
            project(k)

    bounds = ((0, cut), (cut, rank + 8))
    firsts = (1, 2)
    rs_copies = {}
    for turn in (0, 1):
        for part in range(2):
            lo, hi = bounds[part]
            near = firsts[part]
            to = flip(dp, near, n_dp)
            which = flip(dp, 3, n_dp) if turn == 0 else to
            rs_copies[part, turn] = send(
                image.at[which, lo:hi], rs_in.at[turn, lo:hi], rs_s.at[part, turn], rs_r.at[part, turn], (to, ex, core)
            )
    project(order[-1])
    for part in range(2):
        lo, hi = bounds[part]
        far = 3 - firsts[part]
        to = flip(dp, far, n_dp)
        rs_copies[part, 0].wait_recv()
        forward[lo:hi] = image[to, lo:hi] + rs_in[0, lo:hi]
        rs_copies[part, 2] = send(
            forward.at[lo:hi], rs_in.at[2, lo:hi], rs_s.at[part, 2], rs_r.at[part, 2], (to, ex, core)
        )
    for turn in (1, 2):
        for part in range(2):
            rs_copies[part, turn].wait_recv()
    total = image[dp] + rs_in[1] + rs_in[2]
    mine = total[:rank]
    recip = 1.0 / (total[rank:rank + 1] / token_mean + EPSILON)
    scaled = mine * recip
    both = jnp.concatenate([mine, scaled], axis=0)
    small[...] = lax.dot_general(mine, both, (((1,), (1,)), ((), ())), precision=HIGHEST, preferred_element_type=jnp.float32)
    sm_copies = {}
    for k in range(n_dp - 1, 0, -1):
        sm_copies[k] = send(small, small_in.at[k], sm_s.at[k], sm_r.at[k], (flip(dp, k, n_dp), ex, core))
    s_high, s_low = split(scaled)
    s_both = jnp.concatenate([s_high, s_low], axis=0)
    cross = f32_dot(s_both, g_high[...], ((1,), (0,)))
    inner[...] = cross[:rank] + cross[rank:] + f32_dot(s_high, g_low[...], ((1,), (0,)))
    in_copies = {}
    mid = rank // 2
    for part in range(2):
        rows_of = slice(part * mid, part * mid + mid)
        in_copies[part, 0] = send(
            inner.at[rows_of], inner_in.at[0, rows_of], in_s.at[part, 0], in_r.at[part, 0], (flip(dp, firsts[part], n_dp), ex, core)
        )
    left[...] = jnp.concatenate([s_high, s_high, s_low, s_low], axis=0).T
    recips[...] = jnp.broadcast_to(recip, (8, chunk))
    stores = [pltpu.make_async_copy(left, left_hbm, out_sem.at[2]), pltpu.make_async_copy(recips, recip_hbm, out_sem.at[3])]
    for store in stores:
        store.start()

    sums = small[...]
    for k in range(1, n_dp):
        sm_copies[k].wait_recv()
        sums = sums + small_in[k]
    upper, lower_inv, pivots = eliminate(sums[:, :rank])
    for part in range(2):
        rows_of = slice(part * mid, part * mid + mid)
        in_copies[part, 0].wait_recv()
        inner_mid[rows_of] = inner[rows_of] + inner_in[0, rows_of]
        in_copies[part, 1] = send(
            inner_mid.at[rows_of], inner_in.at[1, rows_of], in_s.at[part, 1], in_r.at[part, 1], (flip(dp, 3 - firsts[part], n_dp), ex, core)
        )
    root = lax.rsqrt(pivots)
    transposed = upper * root
    middle = lax.dot_general(transposed * (root * token_mean), transposed, (((0,), (0,)), ((), ())), precision=HIGHEST, preferred_element_type=jnp.float32)
    middle = middle + sums[:, rank:]
    _, mid_inv, mid_pivots = eliminate(middle)
    inverse = lax.dot_general(mid_inv / mid_pivots, mid_inv, (((0,), (0,)), ((), ())), precision=HIGHEST, preferred_element_type=jnp.float32)
    basis[...] = root * lax.dot_general(lower_inv, mine, (((1,), (0,)), ((), ())), precision=HIGHEST, preferred_element_type=jnp.float32)
    stores.append(pltpu.make_async_copy(basis, basis_hbm, out_sem.at[0]))
    stores[2].start()

    loads[5].wait()
    gates = []
    for k in range(n_exp):
        hit = (route_ref[...] == flip(ex, k, n_exp)).astype(jnp.float32)
        gates.append(jnp.sum(hit * gate_ref[...], axis=0, keepdims=True))
    gates8 = jnp.concatenate(gates + [jnp.zeros((8 - n_exp, rows), jnp.float32)], axis=0)
    gate_cols = gates8.T
    combined = jnp.zeros((rows, half), jnp.float32)
    for k in range(n_exp):
        hidden = jnp.zeros((rows, half), jnp.float32)
        for rel in range(2):
            if (k, rel) in ret_copies:
                ret_copies[k, rel].wait_recv()
            hidden = hidden + f32_dot(pickers[k], ret[k, rel], ((0,), (0,)))
        combined = combined + gate_cols[:, k:k + 1] * hidden
    comb[...] = combined.astype(jnp.bfloat16)
    stores.append(pltpu.make_async_copy(comb, comb_hbm, out_sem.at[1]))
    stores[3].start()

    for part in range(2):
        in_copies[part, 1].wait_recv()
    inner_sum = inner_mid[...] + inner_in[1]
    solved[...] = lax.dot_general(inverse, inner_sum, (((1,), (0,)), ((), ())), precision=HIGHEST, preferred_element_type=jnp.float32)
    stores.append(pltpu.make_async_copy(solved, solved_hbm, out_sem.at[4]))
    stores[4].start()
    for group in (tok_copies, ret_copies, rs_copies, sm_copies, in_copies):
        for copy in group.values():
            copy.wait_send()
    for store in stores:
        store.wait()


def apply(grad_hbm, left_hbm, recip_hbm, solved_hbm, comb_hbm, basis_hbm, comb_out, basis_out, result_hbm,
          grad, left, recips, solved, comb, basis, sem, out_sem):
    chunk = grad.shape[0]
    block = 128
    small = [(solved_hbm, solved), (recip_hbm, recips), (left_hbm, left), (comb_hbm, comb), (basis_hbm, basis)]
    loads = [pltpu.make_async_copy(src, dst, sem.at[i]) for i, (src, dst) in enumerate(small)]
    for c in range(0, chunk, block):
        loads.append(pltpu.make_async_copy(grad_hbm.at[c:c + block], grad.at[c:c + block], sem.at[len(loads)]))
    for load in loads:
        load.start()
    loads[0].wait()
    v_high, v_low = split(solved[...])
    right = jnp.concatenate([v_high, v_low, v_high, v_low], axis=0)
    loads[1].wait()
    recip_cols = recips[...].T
    loads[2].wait()
    stores = []
    for i, c in enumerate(range(0, chunk, block)):
        loads[5 + i].wait()
        grad[c:c + block] = grad[c:c + block] * recip_cols[c:c + block, :1] - f32_dot(left[c:c + block], right, ((1,), (0,)))
        stores.append(pltpu.make_async_copy(grad.at[c:c + block], result_hbm.at[c:c + block], out_sem.at[i]))
        stores[-1].start()
    for i, (src, dst) in enumerate(((comb, comb_out), (basis, basis_out))):
        loads[3 + i].wait()
        stores.append(pltpu.make_async_copy(src, dst, out_sem.at[chunk // block + i]))
        stores[-1].start()
    for store in stores:
        store.wait()


def fast(sizes, tokens, routing, gate_values, expert_weight, subspace, gradient):
    n_dp, n_exp = sizes["dp"], sizes["expert"]
    rows, width = tokens.shape
    choices = routing.shape[1]
    cap = rows * choices // n_exp * 9 // 8
    cap = -(-cap // 8) * 8
    rank = subspace.shape[1]
    hidden = expert_weight.shape[2]
    half = hidden // 2
    chunk = width // n_dp
    token_mean = float(rows * choices * n_dp)
    f32, b16 = jnp.float32, jnp.bfloat16
    hbm = pl.BlockSpec(memory_space=pl.ANY)
    vmem = pl.BlockSpec(memory_space=pltpu.VMEM)
    dma = pltpu.SemaphoreType.DMA
    combined, basis, left, recip, solved = pl.pallas_call(
        functools.partial(exchange, n_dp, n_exp, cap, token_mean),
        out_shape=(
            jax.ShapeDtypeStruct((rows, half), b16),
            jax.ShapeDtypeStruct((rank, chunk), f32),
            jax.ShapeDtypeStruct((chunk, 4 * rank), b16),
            jax.ShapeDtypeStruct((8, chunk), f32),
            jax.ShapeDtypeStruct((rank, hidden), f32),
        ),
        in_specs=[hbm] * 6,
        out_specs=(hbm,) * 5,
        scratch_shapes=[
            pltpu.VMEM((rows, width), b16),
            pltpu.VMEM((choices, rows), jnp.int32),
            pltpu.VMEM((choices, rows), f32),
            pltpu.VMEM((rank, width), b16),
            pltpu.VMEM((width, hidden), b16),
            pltpu.VMEM((chunk, hidden), f32),
            pltpu.VMEM((chunk, hidden), b16),
            pltpu.VMEM((chunk, hidden), b16),
            pltpu.VMEM((n_exp - 1, cap, width), b16),
            pltpu.VMEM((n_exp, cap, width), b16),
            pltpu.VMEM((n_exp, 2, cap, half), b16),
            pltpu.VMEM((n_exp, 2, cap, half), b16),
            pltpu.VMEM((n_dp, rank + 8, chunk), f32),
            pltpu.VMEM((rank + 8, chunk), f32),
            pltpu.VMEM((3, rank + 8, chunk), f32),
            pltpu.VMEM((rank, 2 * rank), f32),
            pltpu.VMEM((n_dp, rank, 2 * rank), f32),
            pltpu.VMEM((rank, hidden), f32),
            pltpu.VMEM((rank, hidden), f32),
            pltpu.VMEM((2, rank, hidden), f32),
            pltpu.VMEM((chunk, 4 * rank), b16),
            pltpu.VMEM((rows, half), b16),
            pltpu.VMEM((rank, chunk), f32),
            pltpu.VMEM((8, chunk), f32),
            pltpu.VMEM((rank, hidden), f32),
            dma((6,)), dma((5,)), dma((n_exp,)), dma((n_exp,)), dma((n_exp, 2)), dma((n_exp, 2)),
            dma((2, 3)), dma((2, 3)), dma((n_dp,)), dma((n_dp,)), dma((2, 2)), dma((2, 2)),
        ],
        compiler_params=pltpu.CompilerParams(
            collective_id=0, has_side_effects=True, vmem_limit_bytes=67000000
        ),
    )(tokens, routing.T, gate_values.T, expert_weight[0], subspace[0], gradient[0, 0])
    combined, basis, result = pl.pallas_call(
        apply,
        out_shape=(
            jax.ShapeDtypeStruct((rows, half), b16),
            jax.ShapeDtypeStruct((rank, chunk), f32),
            jax.ShapeDtypeStruct((chunk, hidden), f32),
        ),
        in_specs=[hbm] * 6,
        out_specs=(hbm,) * 3,
        scratch_shapes=[
            pltpu.VMEM((chunk, hidden), f32),
            pltpu.VMEM((chunk, 4 * rank), b16),
            pltpu.VMEM((8, chunk), f32),
            pltpu.VMEM((rank, hidden), f32),
            pltpu.VMEM((rows, half), b16),
            pltpu.VMEM((rank, chunk), f32),
            dma((5 + chunk // 128,)), dma((2 + chunk // 128,)),
        ],
        compiler_params=pltpu.CompilerParams(vmem_limit_bytes=67000000),
    )(gradient[0, 0], left, recip, solved, combined, basis)
    return (combined, basis[None, None], result[None, None])


def solution(mesh):
    in_specs = (
        P(("dp", "expert"), "tensor"),
        P(("dp", "expert"), None),
        P(("dp", "expert"), None),
        P("expert", "tensor", None),
        P("expert", None, "tensor"),
        P("expert", "tensor", "dp", None),
    )
    out_specs = (
        P(("dp", "expert"), "tensor"),
        P("expert", "tensor", None, "dp"),
        P("expert", "tensor", "dp", None),
    )

    def run(tokens, routing, gate_values, expert_weight, subspace, gradient):
        sizes = dict(mesh.shape)
        if fits(sizes, tokens, subspace, gradient, expert_weight):
            return fast(sizes, tokens, routing, gate_values, expert_weight, subspace, gradient)
        return body(tokens, routing, gate_values, expert_weight, subspace, gradient)

    return jax.shard_map(run, mesh=mesh, in_specs=in_specs, out_specs=out_specs, check_vma=False)
```

```python
import functools

import jax
import jax.numpy as jnp
from jax import lax
from jax.experimental import pallas as pl
from jax.experimental.pallas import tpu as pltpu
from jax.sharding import PartitionSpec as P

EPSILON = 1e-05


def tri_solve(factor, rhs, flip):
    return lax.linalg.triangular_solve(factor, rhs, left_side=True, lower=True, transpose_a=flip)


def finish(image_mine, diagonal, grad_rows, gram_matrix, curvature, inner_term, token_mean):
    highest = lax.Precision.HIGHEST
    factor_low = jnp.linalg.cholesky(gram_matrix)
    eigen_scale = jnp.diagonal(factor_low) / token_mean
    middle = jnp.dot(factor_low / eigen_scale[None, :], factor_low.T, precision=highest) + curvature
    factor_mid = jnp.linalg.cholesky(middle)
    solved = tri_solve(factor_mid, tri_solve(factor_mid, inner_term, False), True)
    scaled = image_mine / diagonal[None, :]
    result = grad_rows / diagonal[:, None] - jnp.dot(scaled.T, solved, precision=highest)
    basis_out = tri_solve(factor_low, image_mine, False)
    return (basis_out, result)


def body(tokens, routing, gate_values, expert_weight, subspace, gradient):
    highest = lax.Precision.HIGHEST
    tok_rows, half_width = tokens.shape
    choose_count = routing.shape[1]
    owners = lax.axis_size("expert")
    tensor_count = lax.axis_size("tensor")
    capacity = tok_rows * choose_count // owners * 9 // 8
    pair_count = tok_rows * choose_count
    slot_count = owners * capacity
    hidden_units = expert_weight.shape[2]
    flat_ids = routing.reshape(pair_count)
    one_hot = (flat_ids[:, None] == jnp.arange(owners, dtype=jnp.int32)[None, :]).astype(
        jnp.float32
    )
    pair_index = jnp.arange(pair_count, dtype=jnp.int32)
    strict_lower = (pair_index[:, None] > pair_index[None, :]).astype(jnp.float32)
    before = jnp.dot(strict_lower, one_hot, preferred_element_type=jnp.float32)
    position = jnp.sum(before * one_hot, axis=1).astype(jnp.int32)
    slot_ids = flat_ids * capacity + position
    matches = (jnp.arange(slot_count, dtype=jnp.int32)[:, None] == slot_ids[None, :]).reshape(
        slot_count, tok_rows, choose_count
    )
    picker = jnp.sum(matches.astype(jnp.float32), axis=2).astype(jnp.bfloat16)
    outgoing = jnp.dot(picker, tokens, preferred_element_type=jnp.float32).astype(jnp.bfloat16)
    outgoing = outgoing.reshape(owners, capacity, half_width)
    incoming = lax.all_to_all(outgoing, "expert", split_axis=0, concat_axis=0, tiled=True)
    slab_rows = incoming.reshape(slot_count, half_width)
    partial_value = jnp.dot(slab_rows, expert_weight[0], preferred_element_type=jnp.float32).astype(
        jnp.bfloat16
    )
    shaped = partial_value.reshape(owners, capacity, tensor_count, hidden_units // tensor_count)
    returned = lax.all_to_all(
        lax.all_to_all(shaped, "expert", split_axis=0, concat_axis=0, tiled=True),
        "tensor",
        split_axis=2,
        concat_axis=2,
        tiled=True,
    )
    hidden = jnp.sum(returned.astype(jnp.float32), axis=2).reshape(
        slot_count, hidden_units // tensor_count
    )
    weighting = jnp.sum(matches.astype(jnp.float32) * gate_values[None, :, :], axis=2).T
    combined = jnp.dot(weighting, hidden, precision=highest).astype(jnp.bfloat16)
    projected = lax.dot_general(
        slab_rows, subspace[0], (((1,), (1,)), ((), ())), preferred_element_type=jnp.float32
    ).astype(jnp.bfloat16)
    image_rows = lax.dot_general(
        projected, slab_rows, (((0,), (0,)), ((), ())), preferred_element_type=jnp.float32
    )
    square_sums = jnp.sum(jnp.square(slab_rows.astype(jnp.float32)), axis=0)
    stacked = jnp.concatenate([image_rows, square_sums[None, :]], axis=0)
    rank_rows = image_rows.shape[0]
    token_mean = float(tok_rows * choose_count * lax.axis_size("dp"))
    grad_rows = gradient[0, 0]
    summed = lax.psum_scatter(stacked, "dp", scatter_dimension=1, tiled=True)
    image_mine = summed[:rank_rows]
    diagonal = summed[rank_rows] / token_mean + EPSILON
    scaled = image_mine / diagonal[None, :]
    gram_part = jnp.dot(image_mine, image_mine.T, precision=highest)
    curve_part = jnp.dot(scaled, image_mine.T, precision=highest)
    inner_part = jnp.dot(scaled, grad_rows, precision=highest)
    gram_matrix, curvature, inner_term = lax.psum((gram_part, curve_part, inner_part), "dp")
    basis_out, result = finish(
        image_mine, diagonal, grad_rows, gram_matrix, curvature, inner_term, token_mean
    )
    return (combined, basis_out[None, None], result[None, None])


HIGHEST = lax.Precision.HIGHEST
MESH = pl.DeviceIdType.MESH


def is_power(n):
    return n & (n - 1) == 0


def fits(sizes, tokens, subspace, gradient, expert_weight):
    few = sizes["dp"] == 4 and sizes["expert"] == 4 and sizes["tensor"] == 2
    even = is_power(sizes["expert"])
    lanes = gradient.shape[2] % 128 == 0 and expert_weight.shape[2] % 256 == 0
    return few and even and lanes and subspace.shape[1] == 64 and tokens.shape[0] == 128


def flip(index, k, n):
    out, bit = 0, 1
    while bit < n:
        own = lax.rem(index // bit, 2)
        out = out + bit * (1 - own if (k // bit) % 2 else own)
        bit *= 2
    return out


def split(x):
    high = x.astype(jnp.bfloat16)
    low = (x - high.astype(jnp.float32)).astype(jnp.bfloat16)
    return high, low


def f32_dot(a, b, dims):
    return lax.dot_general(a, b, (dims, ((), ())), preferred_element_type=jnp.float32)


def eliminate(matrix):
    rank = matrix.shape[0]
    row_id = lax.broadcasted_iota(jnp.int32, (rank, 2 * rank), 0)
    eye = (lax.broadcasted_iota(jnp.int32, (rank, rank), 0) == lax.broadcasted_iota(jnp.int32, (rank, rank), 1)).astype(jnp.float32)
    state = jnp.concatenate([matrix, eye], axis=1)
    group = 8
    for j in range(0, rank, group):
        cols = [jnp.broadcast_to(state[:, j + i:j + i + 1], (rank, 2 * rank)) for i in range(group)]
        rows = [state[j + i:j + i + 1, :] for i in range(group)]
        delta = None
        for i in range(group):
            inverse = 1.0 / cols[i][j + i:j + i + 1, :]
            factor = jnp.where(row_id > j + i, cols[i] * inverse, 0.0)
            for m in range(i + 1, group):
                ratio = cols[i][j + m:j + m + 1, :] * inverse
                rows[m] = rows[m] - ratio * rows[i]
                cols[m] = cols[m] - cols[i] * ratio
            term = factor * rows[i]
            delta = term if delta is None else delta + term
        state = state - delta
    return state[:, :rank], state[:, rank:], jnp.sum(state[:, :rank] * eye, axis=1, keepdims=True)


def exchange(n_dp, n_exp, cap, token_mean, tok_hbm, route_hbm, gate_hbm, w_hbm, sub_hbm, grad_hbm,
             comb_hbm, basis_hbm, left_hbm, recip_hbm, solved_hbm,
             tok, route_ref, gate_ref, sub, wgt, grad, g_high, g_low, out_rows, in_rows, parts, ret, image, forward, rs_in,
             small, small_in, inner, inner_mid, inner_in, left, comb, basis, recips, solved,
             out_last, in_last, fwd_in, p_out, p_in,
             loc_sem, out_sem, tok_s, tok_r, ret_s, ret_r, rs_s, rs_r, sm_s, sm_r, in_s, in_r,
             last_s, last_r, fwd_s, fwd_r, p_s, p_r):
    dp = lax.axis_index("dp")
    ex = lax.axis_index("expert")
    core = lax.axis_index("tensor")
    half = parts.shape[3]
    width = tok.shape[1]
    chunk = width // n_dp
    rank = sub.shape[0]
    rows = tok.shape[0]
    cut = (rank + 8) // 16 * 8 + 8 * ((rank + 8) // 8 % 2)

    loads = [
        pltpu.make_async_copy(tok_hbm, tok, loc_sem.at[0]),
        pltpu.make_async_copy(sub_hbm, sub, loc_sem.at[1]),
        pltpu.make_async_copy(w_hbm, wgt, loc_sem.at[2]),
        pltpu.make_async_copy(grad_hbm, grad, loc_sem.at[3]),
        pltpu.make_async_copy(route_hbm, route_ref, loc_sem.at[4]),
        pltpu.make_async_copy(gate_hbm, gate_ref, loc_sem.at[5]),
    ]
    for i in (4, 0, 1, 5, 2, 3):
        loads[i].start()

    barrier = pltpu.get_barrier_semaphore()
    peers = [(dp, flip(ex, k, n_exp), core) for k in range(1, n_exp)]
    peers += [(dp, flip(ex, k, n_exp), 1 - core) for k in range(n_exp)]
    peers += [(flip(dp, k, n_dp), ex, core) for k in range(1, n_dp)]
    for peer in peers:
        pl.semaphore_signal(barrier, inc=1, device_id=peer, device_id_type=MESH)

    row_i = lax.broadcasted_iota(jnp.int32, (rows, rows), 0)
    col_i = lax.broadcasted_iota(jnp.int32, (rows, rows), 1)
    earlier = (row_i < col_i).astype(jnp.float32)
    slot_i = lax.broadcasted_iota(jnp.int32, (cap, rows), 0)
    loads[4].wait()
    named = []
    for k in range(n_exp):
        hit = route_ref[...] == flip(ex, k, n_exp)
        named.append(jnp.sum(hit.astype(jnp.float32), axis=0, keepdims=True))
    named8 = jnp.concatenate(named + [jnp.zeros((8 - n_exp, rows), jnp.float32)], axis=0)
    before = f32_dot(named8.astype(jnp.bfloat16), earlier.astype(jnp.bfloat16), ((1,), (0,)))

    def picker(k):
        place = before[k:k + 1].astype(jnp.int32)
        return jnp.where((slot_i == place) & (named8[k:k + 1] > 0.5), 1.0, 0.0).astype(jnp.bfloat16)

    pickers = [picker(k) for k in range(n_exp)]
    loads[0].wait()
    pl.semaphore_wait(barrier, len(peers))

    sends = []

    def send(src, dst, s, r, peer):
        copy = pltpu.make_async_remote_copy(
            src_ref=src, dst_ref=dst, send_sem=s, recv_sem=r, device_id=peer, device_id_type=MESH
        )
        copy.start()
        return copy

    tok_copies = {}
    last = n_exp // 2
    turns = (3, 1, 2, 0)
    last_copies, fwd_copies, p_copies = {}, {}, {}

    def columns(kd):
        return pl.ds(pl.multiple_of(flip(dp, kd, n_dp) * chunk, 128), chunk)

    for k in list(range(n_exp - 1, 0, -1)):
        if k == last:
            for kd in turns:
                out_last[kd] = f32_dot(pickers[k], tok[:, columns(kd)], ((1,), (0,))).astype(jnp.bfloat16)
                last_copies[kd] = send(out_last.at[kd], in_last.at[kd], last_s.at[kd], last_r.at[kd], (dp, flip(ex, k, n_exp), core))
            continue
        out_rows[k // 2] = f32_dot(pickers[k], tok[...], ((1,), (0,))).astype(jnp.bfloat16)
        tok_copies[k] = send(out_rows.at[k // 2], in_rows.at[k], tok_s.at[k], tok_r.at[k], (dp, flip(ex, k, n_exp), core))
    in_rows[0] = f32_dot(pickers[0], tok[...], ((1,), (0,))).astype(jnp.bfloat16)
    loads[1].wait()

    def add_image(k):
        got = in_rows.at[k]
        projected = f32_dot(got[...], sub[...], ((1,), (1,))).astype(jnp.bfloat16)
        for j in range(n_dp):
            part = got[:, j * chunk:(j + 1) * chunk]
            img = f32_dot(projected, part, ((0,), (0,)))
            wide = part.astype(jnp.float32)
            sq = jnp.sum(wide * wide, axis=0, keepdims=True)
            if k == 0:
                image[j, :rank] = img
                image[j, rank:rank + 8] = jnp.broadcast_to(sq, (8, chunk))
            else:
                image[j, :rank] += img
                image[j, rank:rank + 8] += jnp.broadcast_to(sq, (8, chunk))

    ret_copies = {}

    def project(k):
        for rel in range(2):
            which = core if rel == 0 else 1 - core
            cols = pl.ds(pl.multiple_of(which * half, half), half)
            value = f32_dot(in_rows[k], wgt[:, cols], ((1,), (0,))).astype(jnp.bfloat16)
            if k == 0 and rel == 0:
                ret[0, 0] = value
            else:
                parts[k, rel] = value
                peer = (dp, flip(ex, k, n_exp), which)
                ret_copies[k, rel] = send(parts.at[k, rel], ret.at[k, rel], ret_s.at[k, rel], ret_r.at[k, rel], peer)

    add_image(0)
    loads[2].wait()
    project(0)
    loads[3].wait()
    high, low = split(grad[...])
    g_high[...] = high
    g_low[...] = low
    order = [k for k in range(1, n_exp) if k != last]
    for k in order:
        tok_copies[k].wait_recv()
        add_image(k)
        if k != order[-1]:
            project(k)

    bounds = ((0, cut), (cut, rank + 8))
    firsts = (1, 2)
    rs_copies = {}
    for turn in (0, 1):
        for part in range(2):
            lo, hi = bounds[part]
            near = firsts[part]
            to = flip(dp, near, n_dp)
            which = flip(dp, 3, n_dp) if turn == 0 else to
            rs_copies[part, turn] = send(
                image.at[which, lo:hi], rs_in.at[turn, lo:hi], rs_s.at[part, turn], rs_r.at[part, turn], (to, ex, core)
            )
    project(order[-1])
    for part in range(2):
        lo, hi = bounds[part]
        far = 3 - firsts[part]
        to = flip(dp, far, n_dp)
        rs_copies[part, 0].wait_recv()
        forward[lo:hi] = image[to, lo:hi] + rs_in[0, lo:hi]
        rs_copies[part, 2] = send(
            forward.at[lo:hi], rs_in.at[2, lo:hi], rs_s.at[part, 2], rs_r.at[part, 2], (to, ex, core)
        )

    half_cols = [pl.ds(pl.multiple_of((core if rel == 0 else 1 - core) * half, half), half) for rel in range(2)]
    projected = jnp.zeros((cap, rank), jnp.float32)
    sums2 = [jnp.zeros((cap, half), jnp.float32) for _ in range(2)]

    def add_products(kd):
        at = pl.ds(pl.multiple_of(flip(dp, kd, n_dp) * chunk, 128), chunk)
        for rel in range(2):
            sums2[rel] = sums2[rel] + f32_dot(in_last[kd], wgt[at, half_cols[rel]], ((1,), (0,)))

    for kd in turns:
        last_copies[kd].wait_recv()
        if kd:
            fwd_copies[kd] = send(in_last.at[kd], fwd_in.at[kd], fwd_s.at[kd], fwd_r.at[kd], (flip(dp, kd, n_dp), ex, core))
        projected = projected + f32_dot(in_last[kd], sub[:, columns(kd)], ((1,), (1,)))
        if kd != turns[-1]:
            add_products(kd)
    p_out[...] = jnp.concatenate([projected, jnp.zeros((cap, 128 - rank), jnp.float32)], axis=1).astype(jnp.bfloat16)
    for kd in range(n_dp - 1, 0, -1):
        p_copies[kd] = send(p_out, p_in.at[kd], p_s.at[kd], p_r.at[kd], (flip(dp, kd, n_dp), ex, core))
    add_products(turns[-1])
    for rel in range(2):
        parts[last, rel] = sums2[rel].astype(jnp.bfloat16)
        peer = (dp, flip(ex, last, n_exp), core if rel == 0 else 1 - core)
        ret_copies[last, rel] = send(parts.at[last, rel], ret.at[last, rel], ret_s.at[last, rel], ret_r.at[last, rel], peer)

    for turn in (1, 2):
        for part in range(2):
            rs_copies[part, turn].wait_recv()
    total = image[dp] + rs_in[1] + rs_in[2]
    mine = total[:rank]
    squares = total[rank:rank + 1]
    for kd in range(n_dp):
        if kd:
            fwd_copies[kd].wait_recv()
            p_copies[kd].wait_recv()
        part_rows = fwd_in[kd] if kd else in_last[0]
        mine = mine + f32_dot(p_in[kd] if kd else p_out[...], part_rows, ((0,), (0,)))[:rank]
        wide = part_rows.astype(jnp.float32)
        squares = squares + jnp.sum(wide * wide, axis=0, keepdims=True)
    recip = 1.0 / (squares / token_mean + EPSILON)
    scaled = mine * recip
    both = jnp.concatenate([mine, scaled], axis=0)
    small[...] = lax.dot_general(mine, both, (((1,), (1,)), ((), ())), precision=HIGHEST, preferred_element_type=jnp.float32)
    sm_copies = {}
    for k in range(n_dp - 1, 0, -1):
        sm_copies[k] = send(small, small_in.at[k], sm_s.at[k], sm_r.at[k], (flip(dp, k, n_dp), ex, core))
    s_high, s_low = split(scaled)
    s_both = jnp.concatenate([s_high, s_low], axis=0)
    cross = f32_dot(s_both, g_high[...], ((1,), (0,)))
    inner[...] = cross[:rank] + cross[rank:] + f32_dot(s_high, g_low[...], ((1,), (0,)))
    in_copies = {}
    mid = rank // 2
    for part in range(2):
        rows_of = slice(part * mid, part * mid + mid)
        in_copies[part, 0] = send(
            inner.at[rows_of], inner_in.at[0, rows_of], in_s.at[part, 0], in_r.at[part, 0], (flip(dp, firsts[part], n_dp), ex, core)
        )
    left[...] = jnp.concatenate([s_high, s_high, s_low, s_low], axis=0).T
    recips[...] = jnp.broadcast_to(recip, (8, chunk))
    stores = [pltpu.make_async_copy(left, left_hbm, out_sem.at[2]), pltpu.make_async_copy(recips, recip_hbm, out_sem.at[3])]
    for store in stores:
        store.start()

    sums = small[...]
    for k in range(1, n_dp):
        sm_copies[k].wait_recv()
        sums = sums + small_in[k]
    upper, lower_inv, pivots = eliminate(sums[:, :rank])
    for part in range(2):
        rows_of = slice(part * mid, part * mid + mid)
        in_copies[part, 0].wait_recv()
        inner_mid[rows_of] = inner[rows_of] + inner_in[0, rows_of]
        in_copies[part, 1] = send(
            inner_mid.at[rows_of], inner_in.at[1, rows_of], in_s.at[part, 1], in_r.at[part, 1], (flip(dp, 3 - firsts[part], n_dp), ex, core)
        )
    root = lax.rsqrt(pivots)
    transposed = upper * root
    middle = lax.dot_general(transposed * (root * token_mean), transposed, (((0,), (0,)), ((), ())), precision=HIGHEST, preferred_element_type=jnp.float32)
    middle = middle + sums[:, rank:]
    _, mid_inv, mid_pivots = eliminate(middle)
    inverse = lax.dot_general(mid_inv / mid_pivots, mid_inv, (((0,), (0,)), ((), ())), precision=HIGHEST, preferred_element_type=jnp.float32)
    basis[...] = root * lax.dot_general(lower_inv, mine, (((1,), (0,)), ((), ())), precision=HIGHEST, preferred_element_type=jnp.float32)
    stores.append(pltpu.make_async_copy(basis, basis_hbm, out_sem.at[0]))
    stores[2].start()

    loads[5].wait()
    gates = []
    for k in range(n_exp):
        hit = (route_ref[...] == flip(ex, k, n_exp)).astype(jnp.float32)
        gates.append(jnp.sum(hit * gate_ref[...], axis=0, keepdims=True))
    gates8 = jnp.concatenate(gates + [jnp.zeros((8 - n_exp, rows), jnp.float32)], axis=0)
    gate_cols = gates8.T
    combined = jnp.zeros((rows, half), jnp.float32)
    for k in range(n_exp):
        hidden = jnp.zeros((rows, half), jnp.float32)
        for rel in range(2):
            if (k, rel) in ret_copies:
                ret_copies[k, rel].wait_recv()
            hidden = hidden + f32_dot(pickers[k], ret[k, rel], ((0,), (0,)))
        combined = combined + gate_cols[:, k:k + 1] * hidden
    comb[...] = combined.astype(jnp.bfloat16)
    stores.append(pltpu.make_async_copy(comb, comb_hbm, out_sem.at[1]))
    stores[3].start()

    for part in range(2):
        in_copies[part, 1].wait_recv()
    inner_sum = inner_mid[...] + inner_in[1]
    solved[...] = lax.dot_general(inverse, inner_sum, (((1,), (0,)), ((), ())), precision=HIGHEST, preferred_element_type=jnp.float32)
    stores.append(pltpu.make_async_copy(solved, solved_hbm, out_sem.at[4]))
    stores[4].start()
    for group in (last_copies, fwd_copies, p_copies, tok_copies, ret_copies, rs_copies, sm_copies, in_copies):
        for copy in group.values():
            copy.wait_send()
    for store in stores:
        store.wait()


def apply(grad_hbm, left_hbm, recip_hbm, solved_hbm, comb_hbm, basis_hbm, comb_out, basis_out, result_hbm,
          grad, left, recips, solved, comb, basis, sem, out_sem):
    chunk = grad.shape[0]
    block = 128
    small = [(solved_hbm, solved), (recip_hbm, recips), (left_hbm, left), (comb_hbm, comb), (basis_hbm, basis)]
    loads = [pltpu.make_async_copy(src, dst, sem.at[i]) for i, (src, dst) in enumerate(small)]
    for c in range(0, chunk, block):
        loads.append(pltpu.make_async_copy(grad_hbm.at[c:c + block], grad.at[c:c + block], sem.at[len(loads)]))
    for load in loads:
        load.start()
    loads[0].wait()
    v_high, v_low = split(solved[...])
    right = jnp.concatenate([v_high, v_low, v_high, v_low], axis=0)
    loads[1].wait()
    recip_cols = recips[...].T
    loads[2].wait()
    stores = []
    for i, c in enumerate(range(0, chunk, block)):
        loads[5 + i].wait()
        grad[c:c + block] = grad[c:c + block] * recip_cols[c:c + block, :1] - f32_dot(left[c:c + block], right, ((1,), (0,)))
        stores.append(pltpu.make_async_copy(grad.at[c:c + block], result_hbm.at[c:c + block], out_sem.at[i]))
        stores[-1].start()
    for i, (src, dst) in enumerate(((comb, comb_out), (basis, basis_out))):
        loads[3 + i].wait()
        stores.append(pltpu.make_async_copy(src, dst, out_sem.at[chunk // block + i]))
        stores[-1].start()
    for store in stores:
        store.wait()


def fast(sizes, tokens, routing, gate_values, expert_weight, subspace, gradient):
    n_dp, n_exp = sizes["dp"], sizes["expert"]
    rows, width = tokens.shape
    choices = routing.shape[1]
    cap = rows * choices // n_exp * 9 // 8
    cap = -(-cap // 8) * 8
    rank = subspace.shape[1]
    hidden = expert_weight.shape[2]
    half = hidden // 2
    chunk = width // n_dp
    token_mean = float(rows * choices * n_dp)
    f32, b16 = jnp.float32, jnp.bfloat16
    hbm = pl.BlockSpec(memory_space=pl.ANY)
    vmem = pl.BlockSpec(memory_space=pltpu.VMEM)
    dma = pltpu.SemaphoreType.DMA
    combined, basis, left, recip, solved = pl.pallas_call(
        functools.partial(exchange, n_dp, n_exp, cap, token_mean),
        out_shape=(
            jax.ShapeDtypeStruct((rows, half), b16),
            jax.ShapeDtypeStruct((rank, chunk), f32),
            jax.ShapeDtypeStruct((chunk, 4 * rank), b16),
            jax.ShapeDtypeStruct((8, chunk), f32),
            jax.ShapeDtypeStruct((rank, hidden), f32),
        ),
        in_specs=[hbm] * 6,
        out_specs=(hbm,) * 5,
        scratch_shapes=[
            pltpu.VMEM((rows, width), b16),
            pltpu.VMEM((choices, rows), jnp.int32),
            pltpu.VMEM((choices, rows), f32),
            pltpu.VMEM((rank, width), b16),
            pltpu.VMEM((width, hidden), b16),
            pltpu.VMEM((chunk, hidden), f32),
            pltpu.VMEM((chunk, hidden), b16),
            pltpu.VMEM((chunk, hidden), b16),
            pltpu.VMEM((n_exp - 2, cap, width), b16),
            pltpu.VMEM((n_exp, cap, width), b16),
            pltpu.VMEM((n_exp, 2, cap, half), b16),
            pltpu.VMEM((n_exp, 2, cap, half), b16),
            pltpu.VMEM((n_dp, rank + 8, chunk), f32),
            pltpu.VMEM((rank + 8, chunk), f32),
            pltpu.VMEM((3, rank + 8, chunk), f32),
            pltpu.VMEM((rank, 2 * rank), f32),
            pltpu.VMEM((n_dp, rank, 2 * rank), f32),
            pltpu.VMEM((rank, hidden), f32),
            pltpu.VMEM((rank, hidden), f32),
            pltpu.VMEM((2, rank, hidden), f32),
            pltpu.VMEM((chunk, 4 * rank), b16),
            pltpu.VMEM((rows, half), b16),
            pltpu.VMEM((rank, chunk), f32),
            pltpu.VMEM((8, chunk), f32),
            pltpu.VMEM((rank, hidden), f32),
            pltpu.VMEM((n_dp, cap, chunk), b16),
            pltpu.VMEM((n_dp, cap, chunk), b16),
            pltpu.VMEM((n_dp, cap, chunk), b16),
            pltpu.VMEM((cap, 128), b16),
            pltpu.VMEM((n_dp, cap, 128), b16),
            dma((6,)), dma((5,)), dma((n_exp,)), dma((n_exp,)), dma((n_exp, 2)), dma((n_exp, 2)),
            dma((2, 3)), dma((2, 3)), dma((n_dp,)), dma((n_dp,)), dma((2, 2)), dma((2, 2)),
            dma((n_dp,)), dma((n_dp,)), dma((n_dp,)), dma((n_dp,)), dma((n_dp,)), dma((n_dp,)),
        ],
        compiler_params=pltpu.CompilerParams(
            collective_id=0, has_side_effects=True, vmem_limit_bytes=67000000
        ),
    )(tokens, routing.T, gate_values.T, expert_weight[0], subspace[0], gradient[0, 0])
    combined, basis, result = pl.pallas_call(
        apply,
        out_shape=(
            jax.ShapeDtypeStruct((rows, half), b16),
            jax.ShapeDtypeStruct((rank, chunk), f32),
            jax.ShapeDtypeStruct((chunk, hidden), f32),
        ),
        in_specs=[hbm] * 6,
        out_specs=(hbm,) * 3,
        scratch_shapes=[
            pltpu.VMEM((chunk, hidden), f32),
            pltpu.VMEM((chunk, 4 * rank), b16),
            pltpu.VMEM((8, chunk), f32),
            pltpu.VMEM((rank, hidden), f32),
            pltpu.VMEM((rows, half), b16),
            pltpu.VMEM((rank, chunk), f32),
            dma((5 + chunk // 128,)), dma((2 + chunk // 128,)),
        ],
        compiler_params=pltpu.CompilerParams(vmem_limit_bytes=67000000),
    )(gradient[0, 0], left, recip, solved, combined, basis)
    return (combined, basis[None, None], result[None, None])


def solution(mesh):
    in_specs = (
        P(("dp", "expert"), "tensor"),
        P(("dp", "expert"), None),
        P(("dp", "expert"), None),
        P("expert", "tensor", None),
        P("expert", None, "tensor"),
        P("expert", "tensor", "dp", None),
    )
    out_specs = (
        P(("dp", "expert"), "tensor"),
        P("expert", "tensor", None, "dp"),
        P("expert", "tensor", "dp", None),
    )

    def run(tokens, routing, gate_values, expert_weight, subspace, gradient):
        sizes = dict(mesh.shape)
        if fits(sizes, tokens, subspace, gradient, expert_weight):
            return fast(sizes, tokens, routing, gate_values, expert_weight, subspace, gradient)
        return body(tokens, routing, gate_values, expert_weight, subspace, gradient)

    return jax.shard_map(run, mesh=mesh, in_specs=in_specs, out_specs=out_specs, check_vma=False)
```
